32 devices in a mesh: groups: 2 (over y), side: 2 (over core), ffn: 4 (over z), rep: 2 (over x).
Axes of the slice: x: 2, y: 2, z: 4, core: 2. Of those that a mesh axis runs over, the one named last changes fastest.
Arguments:
- queries: bfloat16 [16, 8192], P(('groups', 'side', 'rep')), parts along dimension 0, may hold values from -24 to 24
- key_cache: bfloat16 [16, 3072, 1024], P(('groups', 'side', 'rep'), 'ffn'), parts along dimension 0, may hold values from -4 to 4
- value_cache: bfloat16 [16, 3072, 1024], P(('groups', 'side', 'rep'), 'ffn'), parts along dimension 0, may hold values from -24 to 24
- decoded_key: bfloat16 [16, 1024], P(('groups', 'side', 'rep')), parts along dimension 0, may hold values from -6 to 6
- decoded_value: bfloat16 [16, 1024], P(('groups', 'side', 'rep')), parts along dimension 0, may hold values from -24 to 24
- lengths: int32 [16], P(('groups', 'side', 'rep')), parts along dimension 0, may hold values from 2 to 3072, as said below
- counts: int32 [8], P('groups'), parts along dimension 0, may hold values from 1 to 2, as said below
- residual: bfloat16 [16, 8192], P('groups', ('side', 'ffn', 'rep')), parts along dimension 0, may hold values from -144 to 144
- out_weight: bfloat16 [8192, 8192], P(None, ('side', 'ffn', 'rep')), may hold values from -0.0625 to 0.0625
- norm_gain: bfloat16 [8192], P(('side', 'ffn', 'rep')), may hold values from 0.099609375 to 1.8984375
- gate_weight: bfloat16 [14336, 8192], P('rep', ('side', 'ffn')), may hold values from -0.0625 to 0.0625
- up_weight: bfloat16 [14336, 8192], P('rep', ('side', 'ffn')), may hold values from -0.0625 to 0.0625
- down_weight: bfloat16 [14336, 8192], P('rep', ('side', 'ffn')), may hold values from -0.046875 to 0.046875
Outputs:
- layer_out: bfloat16 [16, 8192], P('groups', ('side', 'ffn', 'rep')), parts along dimension 0
The draws below stay inside these ranges and needn't reach their ends.
There are 2 independent parts, one for each index of `groups`. The reference program is written for one: setup_inputs(seed, part) draws one part's arguments, and reference() takes and returns one part's arrays. A program takes and returns all parts, laid end to end along the dimension named above; an argument that names none is the same for every part. Nothing has to cross between parts.
Inputs may be any that keep to these rules, and one draw needn't show every extreme that they name: `lengths`: a request's positions at or past its length are ignored; some request has all 3072 positions in use. `counts`: slots at or past a group's count are unused; some group uses all 2 slots.
All inputs are finite; a program needn't handle non-finite values.
Results may differ from the reference program's by a relative error of at most 0.014.
Values may be sent and summed in bfloat16 or wider, within the bound.
A program may use at most 128 MiB of HBM per device.

```python
import jax
import jax.numpy as jnp
from jax import lax

D = 8192
QUERY_HEADS = 64
KEY_VALUE_HEADS = 8
HEAD_WIDTH = 128
FF = 14336
R_SLOT = 2
CONTEXT_LENGTH = 3072
SLOT_GROUPS = 4
REQUEST_TOTAL = 8


def drawn_pair(key):
    folded = jax.random.fold_in(key, 7)
    key_sample, query_draw = jax.random.split(folded, 2)
    cache_entries = jax.random.truncated_normal(key_sample, -4.0, 4.0, (REQUEST_TOTAL, CONTEXT_LENGTH, KEY_VALUE_HEADS * HEAD_WIDTH), jnp.float32)
    asked = jax.random.truncated_normal(query_draw, -4.0, 4.0, (REQUEST_TOTAL, QUERY_HEADS * HEAD_WIDTH), jnp.float32)
    return (asked, cache_entries)


def draw_queries(key, part):
    return drawn_pair(key)[0].astype(jnp.bfloat16)


def draw_key_cache(key, part):
    return drawn_pair(key)[1].astype(jnp.bfloat16)


def draw_value_cache(key, part):
    noise_draw, sign_draw = jax.random.split(jax.random.fold_in(key, 11))
    channel_sign = jax.random.randint(sign_draw, (1, 1, KEY_VALUE_HEADS * HEAD_WIDTH), 0, 2, dtype=jnp.int32).astype(jnp.float32) * 2.0 - 1.0
    place = jnp.arange(CONTEXT_LENGTH, dtype=jnp.float32).reshape(1, CONTEXT_LENGTH, 1) / (CONTEXT_LENGTH - 1)
    noise = jax.random.truncated_normal(noise_draw, -4.0, 4.0, (REQUEST_TOTAL, CONTEXT_LENGTH, KEY_VALUE_HEADS * HEAD_WIDTH), jnp.float32)
    drawn = 2.0 * noise + channel_sign * (1.0 + 2.0 * place)
    return drawn.astype(jnp.bfloat16)


def draw_lengths(key, part):
    length_draw, pick_draw = jax.random.split(jax.random.fold_in(key, 5))
    drawn = jax.random.randint(length_draw, (REQUEST_TOTAL,), 2, CONTEXT_LENGTH + 1, dtype=jnp.int32)
    chosen = jax.random.randint(pick_draw, (), 0, REQUEST_TOTAL, dtype=jnp.int32)
    return drawn.at[chosen].set(CONTEXT_LENGTH)


def draw_counts(key, part):
    count_draw, pick_draw = jax.random.split(jax.random.fold_in(key, 9))
    drawn = jax.random.randint(count_draw, (SLOT_GROUPS,), 1, R_SLOT + 1, dtype=jnp.int32)
    chosen = jax.random.randint(pick_draw, (), 0, SLOT_GROUPS, dtype=jnp.int32)
    return drawn.at[chosen].set(R_SLOT)


def draw_residual(key, part):
    base_draw = jax.random.fold_in(jax.random.fold_in(key, 3), 0)
    column = jnp.arange(D, dtype=jnp.float32) / (D - 1)
    rising = 1.0 + 2.0 * column
    drawn = jax.random.truncated_normal(base_draw, -4.0, 4.0, (REQUEST_TOTAL, D), jnp.float32) * rising
    return drawn.astype(jnp.bfloat16)


def block_levels(stream_key, dims, shards, low, top_value):
    gain = 1.0
    for axis_at, blocks in shards:
        draws = jax.random.uniform(jax.random.fold_in(jax.random.fold_in(stream_key, 6), axis_at), (blocks,), jnp.float32, low / len(shards), top_value / len(shards))
        gain = gain * jnp.repeat(jnp.exp(draws), dims[axis_at] // blocks).reshape((-1,) + (1,) * (len(dims) - 1 - axis_at))
    return gain


def centred(stream_key, shape, spread, limit, cuts=(), kind=jnp.bfloat16):
    values = spread * jax.random.normal(stream_key, shape, jnp.float32)
    if cuts:
        values = values * block_levels(stream_key, shape, cuts, -0.22, 0.18)
    return jnp.clip(values, -limit, limit).astype(kind)


def setup_inputs(seed: int = 0, part: int = 0) -> dict:
    splits = jax.random.split(jax.random.key(seed), 14)
    part_keys = jax.random.split(jax.random.fold_in(splits[13], part), 14)
    queries = draw_queries(jax.random.fold_in(jax.random.fold_in(splits[13], part), 71), part)
    key_cache = draw_key_cache(jax.random.fold_in(jax.random.fold_in(splits[13], part), 71), part)
    value_cache = draw_value_cache(jax.random.fold_in(jax.random.fold_in(splits[13], part), 71), part)
    decoded_key = centred(part_keys[3], (REQUEST_TOTAL, KEY_VALUE_HEADS * HEAD_WIDTH), 1.0, 6.0, ((0, 4),))
    decoded_value = centred(part_keys[4], (REQUEST_TOTAL, KEY_VALUE_HEADS * HEAD_WIDTH), 4.0, 24.0, ((0, 4),))
    lengths = draw_lengths(jax.random.fold_in(jax.random.fold_in(splits[13], part), 71), part)
    counts = draw_counts(jax.random.fold_in(jax.random.fold_in(splits[13], part), 71), part)
    residual = draw_residual(jax.random.fold_in(jax.random.fold_in(splits[13], part), 71), part)
    out_weight = centred(splits[8], (QUERY_HEADS * HEAD_WIDTH, D), (QUERY_HEADS * HEAD_WIDTH) ** -0.5, 0.0625, ((1, 16),))
    norm_gain = jnp.clip(1.0 + 0.18 * jax.random.normal(splits[9], (D,), jnp.float32), 0.099609375, 1.8984375).astype(jnp.bfloat16)
    gate_weight = centred(splits[10], (FF, D), D ** -0.5, 0.0625, ((0, 2), (1, 8)))
    up_weight = centred(splits[11], (FF, D), D ** -0.5, 0.0625, ((0, 2), (1, 8)))
    down_weight = centred(splits[12], (FF, D), FF ** -0.5, 0.046875, ((0, 2), (1, 8)))
    return dict(queries=queries, key_cache=key_cache, value_cache=value_cache, decoded_key=decoded_key, decoded_value=decoded_value, lengths=lengths, counts=counts, residual=residual, out_weight=out_weight, norm_gain=norm_gain, gate_weight=gate_weight, up_weight=up_weight, down_weight=down_weight)


norm_eps = 1e-05

def attend(request):
    single_query_row, rows_of_key, rows_of_value, current_key, current_value, length = request
    group_width = QUERY_HEADS // KEY_VALUE_HEADS
    logit_scale = HEAD_WIDTH ** (-0.5)
    heads_of_query = single_query_row.astype(jnp.float32).reshape(KEY_VALUE_HEADS, group_width, HEAD_WIDTH)
    heads_of_key = rows_of_key.astype(jnp.float32).reshape(CONTEXT_LENGTH, KEY_VALUE_HEADS, HEAD_WIDTH)
    heads_of_value = rows_of_value.astype(jnp.float32).reshape(CONTEXT_LENGTH, KEY_VALUE_HEADS, HEAD_WIDTH)
    scores = jnp.einsum('hgd,thd->hgt', heads_of_query, heads_of_key) * logit_scale
    current_score = jnp.einsum('ayj,aj->ay', heads_of_query, current_key.astype(jnp.float32).reshape(KEY_VALUE_HEADS, HEAD_WIDTH)) * logit_scale
    in_range = (jnp.arange(CONTEXT_LENGTH, dtype=jnp.int32) < length)[None, None, :]
    peak_score = jnp.maximum(lax.optimization_barrier(jnp.max(jnp.where(in_range, scores, -1e+30), axis=-1)), current_score)
    weights = jnp.where(in_range, jnp.exp(scores - peak_score[..., None]), 0.0)
    fresh_weight = jnp.exp(current_score - peak_score)
    weight_sum = lax.optimization_barrier(jnp.sum(weights, axis=-1)) + fresh_weight
    rounded = lax.optimization_barrier(weights.astype(jnp.bfloat16)).astype(jnp.float32)
    current_rounded = lax.optimization_barrier(fresh_weight.astype(jnp.bfloat16)).astype(jnp.float32)
    weighted_values = jnp.einsum('hgt,thd->hgd', rounded, heads_of_value)
    weighted_values = weighted_values + current_rounded[..., None] * current_value.astype(jnp.float32).reshape(KEY_VALUE_HEADS, 1, HEAD_WIDTH)
    return (weighted_values / weight_sum[..., None]).reshape(QUERY_HEADS * HEAD_WIDTH).astype(jnp.bfloat16)

def reference(queries, key_cache, value_cache, decoded_key, decoded_value, lengths, counts, residual, out_weight, norm_gain, gate_weight, up_weight, down_weight):
    attended = lax.map(attend, (queries, key_cache, value_cache, decoded_key, decoded_value, lengths))
    projected = jnp.dot(attended, out_weight, preferred_element_type=jnp.float32)
    stream = (residual.astype(jnp.float32) + projected).astype(jnp.bfloat16)
    widened = stream.astype(jnp.float32)
    squares = lax.optimization_barrier(jnp.sum(widened * widened, axis=1, keepdims=True))
    normed = (widened * lax.rsqrt(squares / D + norm_eps) * norm_gain.astype(jnp.float32)).astype(jnp.bfloat16)
    contract = (((1,), (1,)), ((), ()))
    gate_proj = lax.dot_general(normed, gate_weight, contract, preferred_element_type=jnp.float32)
    up_proj = lax.dot_general(normed, up_weight, contract, preferred_element_type=jnp.float32)
    hidden = (jax.nn.silu(gate_proj) * up_proj).astype(jnp.bfloat16)
    ffn_out = jnp.dot(hidden, down_weight, preferred_element_type=jnp.float32)
    row_ids = jnp.arange(REQUEST_TOTAL, dtype=jnp.int32)
    active = row_ids % R_SLOT < counts[row_ids // R_SLOT]
    return jnp.where(active[:, None], widened + ffn_out, 0.0).astype(jnp.bfloat16)
```

```python
import functools

import jax
import jax.numpy as jnp
from jax import lax
from jax.experimental import pallas as pl
from jax.experimental.pallas import tpu as pltpu
from jax.sharding import PartitionSpec as P

D = 8192
QUERY_HEADS = 64
KEY_VALUE_HEADS = 8
HEAD_WIDTH = 128
GROUP_WIDTH = QUERY_HEADS // KEY_VALUE_HEADS
OUT_CHUNKS = 4

norm_eps = 1e-05
MESH = pl.DeviceIdType.MESH
NT = (((1,), (1,)), ((), ()))
f32 = jnp.float32
bf16 = jnp.bfloat16


def kernel(
    S, F, R,
    q_ref, dk_ref, dv_ref, len_ref, cnt_ref, res_ref, gain_ref,
    k_hbm, v_hbm, wo_hbm, wg_hbm, wu_hbm, wd_hbm,
    out_ref,
    k_v, v_v, wo_v, wg_v, wu_v, wd_v,
    qbd, acc_buf, stat_buf, att_row, att_buf, att_full,
    y_buf, sq_rep, sq_buf, pre,
    gu_send_a, gu_recv_a, hid_a, gu_send_b, gu_recv_b, hid_b, d_send, d_recv,
    k_sem, v_sem, wo_sem, wg_sem, wu_sem, wd_sem,
    acc_ss, acc_rs, stat_ss, stat_rs, att_ss, att_rs,
    y_ss, y_rs, sqr_ss, sqr_rs, sq_ss, sq_rs,
    gu_ss_a, gu_rs_a, hid_ss_a, hid_rs_a, gu_ss_b, gu_rs_b, hid_ss_b, hid_rs_b, d_ss, d_rs,
):
    s = lax.axis_index("side")
    f = lax.axis_index("ffn")
    r = lax.axis_index("rep")
    PN = S * F
    SR = S * R
    me = s * F + f
    mine = s * R + r
    rows_q = q_ref.shape[0]
    span = k_v.shape[1]
    total_rows, cols = res_ref.shape
    kv_width = KEY_VALUE_HEADS * HEAD_WIDTH
    unit = wg_v.shape[1]
    seg_cols = wg_v.shape[2]
    out_rows = wo_v.shape[1]
    scale = HEAD_WIDTH ** (-0.5)

    def dev(side, ffn, rep):
        return {"side": side, "ffn": ffn, "rep": rep}

    def remote(src, dst, ss, rs, to):
        return pltpu.make_async_remote_copy(
            src_ref=src, dst_ref=dst, send_sem=ss, recv_sem=rs, device_id=to, device_id_type=MESH
        )

    def k_copy(i):
        return pltpu.make_async_copy(k_hbm.at[i], k_v.at[i], k_sem.at[i])

    def v_copy(i):
        return pltpu.make_async_copy(v_hbm.at[i], v_v.at[i], v_sem.at[i])

    def wo_copy(i):
        return pltpu.make_async_copy(
            wo_hbm.at[pl.ds(i * out_rows, out_rows)], wo_v.at[i], wo_sem.at[i]
        )

    def unit_copy(hbm, buf, sem, p):
        at = pl.multiple_of(p * unit, 8)
        return pltpu.make_async_copy(hbm.at[pl.ds(at, unit)], buf.at[p], sem.at[p])

    def far_first(t):
        off = F - 1 - t // S
        side = lax.rem(s + 1 + lax.rem(t, S), S)
        ffn = lax.rem(f + off, F)
        return side, ffn, side * F + ffn

    def near_first(t):
        side = lax.rem(s + lax.rem(t, S), S)
        ffn = lax.rem(f - t // S + F, F)
        return side, ffn, side * F + ffn

    for i in range(rows_q):
        k_copy(i).start()
    for i in range(rows_q):
        v_copy(i).start()
    for i in range(OUT_CHUNKS):
        wo_copy(i).start(priority=1)

    barrier = pltpu.get_barrier_semaphore()
    group = S * F * R
    my_id = me * R + r

    def greet(t, c):
        other = lax.rem(my_id + t, group)
        pl.semaphore_signal(
            barrier,
            inc=1,
            device_id=dev(other // (F * R), lax.rem(other // R, F), lax.rem(other, R)),
            device_id_type=MESH,
        )
        return c

    lax.fori_loop(1, group, greet, 0)

    qbd[...] = jnp.zeros(qbd.shape, f32)
    for i in range(rows_q):
        for h in range(QUERY_HEADS):
            b = h // GROUP_WIDTH
            qbd[i, h : h + 1, b * HEAD_WIDTH : (b + 1) * HEAD_WIDTH] = q_ref[
                i : i + 1, h * HEAD_WIDTH : (h + 1) * HEAD_WIDTH
            ].astype(f32)

    start_pos = f * span
    leading = f == 0
    positions = start_pos + lax.broadcasted_iota(jnp.int32, (QUERY_HEADS, span), 1)
    diag = (
        lax.broadcasted_iota(jnp.int32, (QUERY_HEADS, kv_width), 0) // GROUP_WIDTH
        == lax.broadcasted_iota(jnp.int32, (QUERY_HEADS, kv_width), 1) // HEAD_WIDTH
    )

    def acc_copy(to, slot, i):
        return remote(
            acc_buf.at[slot, i], acc_buf.at[slot, i], acc_ss.at[to, i], acc_rs.at[slot, i],
            dev(s, to, r),
        )

    def stat_copy(to, slot, i):
        return remote(
            stat_buf.at[slot, i], stat_buf.at[slot, i], stat_ss.at[to, i], stat_rs.at[slot, i],
            dev(s, to, r),
        )

    for i in range(rows_q):
        qf = qbd[i]
        fresh = (
            jnp.sum(qf * dk_ref[i : i + 1, :].astype(f32), axis=-1, keepdims=True) * scale
        )
        k_copy(i).wait()
        if i == rows_q - 1:
            def start_gu(t, c):
                _, _, p = far_first(t)
                unit_copy(wg_hbm, wg_v, wg_sem, p).start(priority=1)
                unit_copy(wu_hbm, wu_v, wu_sem, p).start(priority=1)
                return c

            lax.fori_loop(0, PN, start_gu, 0)
        sc = lax.dot_general(qf.astype(bf16), k_v[i], NT, preferred_element_type=f32) * scale
        in_range = positions < len_ref[i]
        peak = jnp.max(jnp.where(in_range, sc, -1e30), axis=-1, keepdims=True)
        peak = jnp.where(leading, jnp.maximum(peak, fresh), peak)
        w = jnp.where(in_range, jnp.exp(sc - peak), 0.0)
        wn = jnp.where(leading, jnp.exp(fresh - peak), 0.0)
        norm = jnp.sum(w, axis=-1, keepdims=True) + wn
        both = jnp.broadcast_to(jnp.concatenate([peak, norm], axis=0), (2 * QUERY_HEADS, 128))
        stat_buf[f, i] = both.T[0:8, :]
        v_copy(i).wait()
        o = jnp.dot(w.astype(bf16), v_v[i], preferred_element_type=f32)
        o = o + wn.astype(bf16).astype(f32) * dv_ref[i : i + 1, :].astype(f32)
        o = jnp.where(diag, o, 0.0)
        part = o[:, :HEAD_WIDTH]
        for b in range(1, KEY_VALUE_HEADS):
            part = part + o[:, b * HEAD_WIDTH : (b + 1) * HEAD_WIDTH]
        acc_buf[f, i] = part.astype(bf16)
        if i == 0:
            pl.semaphore_wait(barrier, group - 1)

        def send_acc(t, c, i=i):
            to = lax.rem(f + t, F)
            stat_copy(to, f, i).start()
            acc_copy(to, f, i).start()
            return c

        lax.fori_loop(1, F, send_acc, 0)

    def start_down(t, c):
        _, _, p = near_first(t)
        unit_copy(wd_hbm, wd_v, wd_sem, p).start(priority=1)
        return c

    lax.fori_loop(0, PN, start_down, 0)

    def att_copy(other, slot, i):
        return remote(
            att_buf.at[slot, i], att_buf.at[slot, i], att_ss.at[other, i], att_rs.at[slot, i],
            dev(other // R, f, lax.rem(other, R)),
        )

    low = lax.broadcasted_iota(jnp.int32, (8, 128), 1) < QUERY_HEADS
    for i in range(rows_q):
        def recv_acc(t, c, i=i):
            src = lax.rem(f + t, F)
            stat_copy(src, src, i).wait_recv()
            acc_copy(src, src, i).wait_recv()
            return c

        lax.fori_loop(1, F, recv_acc, 0)
        stats = [stat_buf[z, i] for z in range(F)]
        top = stats[0]
        for z in range(1, F):
            top = jnp.maximum(top, stats[z])
        factors = [jnp.exp(v - top) for v in stats]
        total = factors[0] * pltpu.roll(stats[0], QUERY_HEADS, 1)
        for z in range(1, F):
            total = total + factors[z] * pltpu.roll(stats[z], QUERY_HEADS, 1)
        total = jnp.where(low, total, 1.0)
        factors = [v / total for v in factors]
        if 8 * F < 128:
            factors.append(jnp.zeros((128 - 8 * F, 128), f32))
        turned = jnp.concatenate(factors, axis=0).T
        attended = turned[:QUERY_HEADS, 0:1] * acc_buf[0, i].astype(f32)
        for z in range(1, F):
            attended = attended + turned[:QUERY_HEADS, 8 * z : 8 * z + 1] * acc_buf[z, i].astype(f32)
        for h in range(QUERY_HEADS):
            att_row[i : i + 1, h * HEAD_WIDTH : (h + 1) * HEAD_WIDTH] = attended[h : h + 1, :]
        att_buf[mine, i] = att_row[i : i + 1, :].astype(bf16)

        def send_att(t, c, i=i):
            att_copy(lax.rem(mine + t, SR), mine, i).start()
            return c

        lax.fori_loop(1, SR, send_att, 0)

    def recv_att(t, c):
        src = lax.rem(mine + t, SR)
        for i in range(rows_q):
            att_copy(src, src, i).wait_recv()
        return c

    lax.fori_loop(1, SR, recv_att, 0)
    for j in range(SR):
        for i in range(rows_q):
            at = j * rows_q + i
            att_full[at : at + 1, :] = att_buf[j, i].astype(f32)
    proj = res_ref[...].astype(f32)
    summed = jnp.zeros((total_rows, cols), f32)
    for i in range(OUT_CHUNKS):
        wo_copy(i).wait()
        summed = summed + jnp.dot(
            att_full[:, i * out_rows : (i + 1) * out_rows].astype(bf16),
            wo_v[i],
            preferred_element_type=f32,
        )
    stream = (proj + summed).astype(bf16).astype(f32)
    y_buf[r] = (stream * gain_ref[...].astype(f32).reshape(1, cols)).astype(bf16)
    sq_rep[r] = jnp.broadcast_to(jnp.sum(stream * stream, axis=1, keepdims=True), (total_rows, 128))

    def y_copy(to, slot):
        return remote(y_buf.at[slot], y_buf.at[slot], y_ss.at[to], y_rs.at[slot], dev(s, f, to))

    def sqr_copy(to, slot):
        return remote(
            sq_rep.at[slot], sq_rep.at[slot], sqr_ss.at[to], sqr_rs.at[slot], dev(s, f, to)
        )

    def send_y(t, c):
        to = lax.rem(r + t, R)
        y_copy(to, r).start()
        sqr_copy(to, r).start()
        return c

    lax.fori_loop(1, R, send_y, 0)

    aligned = cols % 128 == 0
    parts = (
        (0, hid_a.shape[2], gu_send_a, gu_recv_a, gu_ss_a, gu_rs_a, hid_a, hid_ss_a, hid_rs_a),
        (hid_a.shape[2], hid_b.shape[2],
         gu_send_b, gu_recv_b, gu_ss_b, gu_rs_b, hid_b, hid_ss_b, hid_rs_b),
    )
    width_a = hid_a.shape[2]

    def half_of(t, which, lhs):
        _, _, p = far_first(t)
        at = pl.ds(pl.multiple_of(which * cols, 128), cols)
        g = lax.dot_general(lhs, wg_v[p, :width_a, at], NT, preferred_element_type=f32)
        u = lax.dot_general(lhs, wu_v[p, :width_a, at], NT, preferred_element_type=f32)
        return g, u

    early = pre.shape[0] if aligned and R == 2 else 0
    if early:
        own_y = y_buf[r]

        def ahead(t, c):
            _, _, p = far_first(t)
            unit_copy(wg_hbm, wg_v, wg_sem, p).wait()
            unit_copy(wu_hbm, wu_v, wu_sem, p).wait()
            g, u = half_of(t, r, own_y)
            pre[t, 0] = g
            pre[t, 1] = u
            return c

        lax.fori_loop(0, early, ahead, 0)

    def recv_y(t, c):
        src = lax.rem(r + t, R)
        y_copy(src, src).wait_recv()
        sqr_copy(src, src).wait_recv()
        return c

    lax.fori_loop(1, R, recv_y, 0)
    squares = sq_rep[0]
    for j in range(1, R):
        squares = squares + sq_rep[j]
    sq_buf[me] = squares

    def sq_copy(t, own):
        side, ffn, p = far_first(t)
        slot = me if own else p
        return remote(
            sq_buf.at[slot], sq_buf.at[slot], sq_ss.at[p], sq_rs.at[slot], dev(side, ffn, r)
        )

    def send_sq(t, c):
        sq_copy(t, True).start()
        return c

    lax.fori_loop(0, PN - 1, send_sq, 0)

    def place(j):
        a = lax.broadcasted_iota(jnp.int32, (cols, seg_cols), 0)
        b = lax.broadcasted_iota(jnp.int32, (cols, seg_cols), 1)
        return jnp.where(b == a + j * cols, 1.0, 0.0).astype(bf16)

    if aligned:
        segment = jnp.concatenate([y_buf[j] for j in range(R)], axis=1)
    else:
        segment = jnp.zeros((total_rows, seg_cols), f32)
        for j in range(R):
            segment = segment + jnp.dot(y_buf[j], place(j), preferred_element_type=f32)
        segment = segment.astype(bf16)

    def gu_copy(part, t, own):
        _, _, gu_send, gu_recv, gu_ss, gu_rs, _, _, _ = parts[part]
        side, ffn, p = far_first(t)
        slot = me if own else p
        return remote(
            gu_send.at[p], gu_recv.at[slot], gu_ss.at[p], gu_rs.at[slot], dev(side, ffn, r)
        )

    def hand_over(part, t, g, u):
        gu_send = parts[part][2]
        _, _, p = far_first(t)
        gu_send[p, 0] = g.astype(bf16)
        gu_send[p, 1] = u.astype(bf16)

        @pl.when(t < PN - 1)
        def _():
            gu_copy(part, t, True).start()

    if early:
        other_y = y_buf[1 - r]

        def finish(t, c):
            g, u = half_of(t, 1 - r, other_y)
            hand_over(0, t, g + pre[t, 0], u + pre[t, 1])
            return c

        lax.fori_loop(0, early, finish, 0)

    def project(part, wait):
        lo, width = parts[part][:2]

        def step(t, c):
            _, _, p = far_first(t)
            if wait:
                unit_copy(wg_hbm, wg_v, wg_sem, p).wait()
            g = lax.dot_general(segment, wg_v[p, lo : lo + width], NT, preferred_element_type=f32)
            if wait:
                unit_copy(wu_hbm, wu_v, wu_sem, p).wait()
            u = lax.dot_general(segment, wu_v[p, lo : lo + width], NT, preferred_element_type=f32)
            hand_over(part, t, g, u)
            return c

        return step

    def hid_copy(part, t, own):
        hid, hid_ss, hid_rs = parts[part][6:]
        side, ffn, p = far_first(t) if own else near_first(t)
        slot = me if own else p
        return remote(
            hid.at[slot], hid.at[slot], hid_ss.at[p], hid_rs.at[slot], dev(side, ffn, r)
        )

    def activate(part, factor):
        _, _, gu_send, gu_recv, _, _, hid, _, _ = parts[part]

        def gather_sums(t, c):
            g, u = c
            _, _, p = far_first(t)
            gu_copy(part, t, False).wait_recv()
            return g + gu_recv[p, 0].astype(f32), u + gu_recv[p, 1].astype(f32)

        g, u = lax.fori_loop(
            0, PN - 1, gather_sums, (gu_send[me, 0].astype(f32), gu_send[me, 1].astype(f32))
        )
        g = g * factor
        u = u * factor
        hid[me] = (g / (1.0 + jnp.exp(-g)) * u).astype(bf16)

        def send_hid(t, c):
            hid_copy(part, t, True).start()
            return c

        lax.fori_loop(0, PN - 1, send_hid, 0)

    lax.fori_loop(early, PN, project(0, True), 0)
    lax.fori_loop(0, PN // 2, project(1, False), 0)

    def gather_squares(t, c):
        _, _, p = far_first(t)
        sq_copy(t, False).wait_recv()
        return c + sq_buf[p]

    q = lax.fori_loop(0, PN - 1, gather_squares, sq_buf[me])
    factor = lax.rsqrt(q / D + norm_eps)[:, 0:1]
    activate(0, factor)
    lax.fori_loop(PN // 2, PN, project(1, False), 0)
    activate(1, factor)

    def down(part):
        lo, width = parts[part][:2]
        hid = parts[part][6]

        def step(t, c):
            _, _, p = near_first(t)
            if part == 0:
                unit_copy(wd_hbm, wd_v, wd_sem, p).wait()

            @pl.when(t > 0)
            def _():
                hid_copy(part, t, False).wait_recv()

            return c + jnp.dot(hid[p], wd_v[p, lo : lo + width], preferred_element_type=f32)

        return step

    terms = jnp.zeros((total_rows, seg_cols), f32)
    for part in range(2):
        terms = lax.fori_loop(0, PN, down(part), terms, unroll=True)
    terms = terms.astype(bf16)
    for j in range(R):
        if aligned:
            d_send[j] = terms[:, j * cols : (j + 1) * cols]
        else:
            d_send[j] = lax.dot_general(
                terms, place(j), NT, preferred_element_type=f32
            ).astype(bf16)

    def d_copy(to, own):
        return remote(
            d_send.at[to], d_recv.at[r if own else to], d_ss.at[to],
            d_rs.at[r if own else to], dev(s, f, to),
        )

    def send_d(t, c):
        d_copy(lax.rem(r + t, R), True).start()
        return c

    lax.fori_loop(1, R, send_d, 0)

    row = lax.broadcasted_iota(jnp.int32, (total_rows, cols), 0)
    slots = total_rows // cnt_ref.shape[0]
    limit = jnp.zeros((total_rows, cols), jnp.int32)
    for i in range(cnt_ref.shape[0]):
        limit = jnp.where(row // slots == i, cnt_ref[i], limit)
    active = lax.rem(row, slots) < limit

    def recv_d(t, c):
        src = lax.rem(r + t, R)
        d_copy(src, False).wait_recv()
        return c + d_recv[src].astype(f32)

    ffn_out = lax.fori_loop(1, R, recv_d, d_send[r].astype(f32))
    out_ref[...] = jnp.where(active, stream + ffn_out, 0.0).astype(bf16)

    def drain_f(t, c):
        to = lax.rem(f + t, F)
        for i in range(rows_q):
            stat_copy(to, f, i).wait_send()
            acc_copy(to, f, i).wait_send()
        return c

    lax.fori_loop(1, F, drain_f, 0)

    def drain_sr(t, c):
        for i in range(rows_q):
            att_copy(lax.rem(mine + t, SR), mine, i).wait_send()
        return c

    lax.fori_loop(1, SR, drain_sr, 0)

    def drain_r(t, c):
        to = lax.rem(r + t, R)
        y_copy(to, r).wait_send()
        sqr_copy(to, r).wait_send()
        d_copy(to, True).wait_send()
        return c

    lax.fori_loop(1, R, drain_r, 0)

    def drain_p(t, c):
        sq_copy(t, True).wait_send()
        for part in range(2):
            gu_copy(part, t, True).wait_send()
            hid_copy(part, t, True).wait_send()
        return c

    lax.fori_loop(0, PN - 1, drain_p, 0)


def body(S, F, R, queries, key_cache, value_cache, decoded_key, decoded_value, lengths, counts,
         residual, out_weight, norm_gain, gate_weight, up_weight, down_weight):
    rows_q = queries.shape[0]
    span = key_cache.shape[1]
    kv_width = key_cache.shape[2]
    total_rows, cols = residual.shape
    units, seg_cols = gate_weight.shape
    PN, SR = S * F, S * R
    unit = units // PN
    step = 128 if unit % 128 == 0 else 16
    width_a = unit * 4 // 7 // step * step
    widths = (width_a, unit - width_a)
    out_rows = out_weight.shape[0] // OUT_CHUNKS
    dma = pltpu.SemaphoreType.DMA
    vmem = pl.BlockSpec(memory_space=pltpu.VMEM)
    smem = pl.BlockSpec(memory_space=pltpu.SMEM)
    hbm = pl.BlockSpec(memory_space=pl.ANY)
    return pl.pallas_call(
        functools.partial(kernel, S, F, R),
        out_shape=pltpu.VMEM((total_rows, cols), bf16),
        in_specs=[vmem, vmem, vmem, smem, smem, vmem, vmem] + [hbm] * 6,
        out_specs=vmem,
        scratch_shapes=[
            pltpu.VMEM((rows_q, span, kv_width), bf16),
            pltpu.VMEM((rows_q, span, kv_width), bf16),
            pltpu.VMEM((OUT_CHUNKS, out_rows, cols), bf16),
            pltpu.VMEM((PN, unit, seg_cols), bf16),
            pltpu.VMEM((PN, unit, seg_cols), bf16),
            pltpu.VMEM((PN, unit, seg_cols), bf16),
            pltpu.VMEM((rows_q, QUERY_HEADS, kv_width), f32),
            pltpu.VMEM((F, rows_q, QUERY_HEADS, HEAD_WIDTH), bf16),
            pltpu.VMEM((F, rows_q, 8, 128), f32),
            pltpu.VMEM((rows_q, QUERY_HEADS * HEAD_WIDTH), f32),
            pltpu.VMEM((SR, rows_q, 1, QUERY_HEADS * HEAD_WIDTH), bf16),
            pltpu.VMEM((total_rows, QUERY_HEADS * HEAD_WIDTH), f32),
            pltpu.VMEM((R, total_rows, cols), bf16),
            pltpu.VMEM((R, total_rows, 128), f32),
            pltpu.VMEM((PN, total_rows, 128), f32),
            pltpu.VMEM((PN // 2 + 1, 2, total_rows, width_a), f32),
            *[
                pltpu.VMEM(shape, bf16)
                for width in widths
                for shape in (
                    (PN, 2, total_rows, width), (PN, 2, total_rows, width),
                    (PN, total_rows, width),
                )
            ],
            pltpu.VMEM((R, total_rows, cols), bf16),
            pltpu.VMEM((R, total_rows, cols), bf16),
            dma((rows_q,)), dma((rows_q,)), dma((OUT_CHUNKS,)),
            dma((PN,)), dma((PN,)), dma((PN,)),
            dma((F, rows_q)), dma((F, rows_q)), dma((F, rows_q)), dma((F, rows_q)),
            dma((SR, rows_q)), dma((SR, rows_q)),
            dma((R,)), dma((R,)), dma((R,)), dma((R,)), dma((PN,)), dma((PN,)),
            *[dma((PN,)) for _ in range(8)], dma((R,)), dma((R,)),
        ],
        compiler_params=pltpu.CompilerParams(
            collective_id=0, has_side_effects=True, vmem_limit_bytes=65000000
        ),
        name="decode_step",
    )(queries, decoded_key, decoded_value, lengths, counts, residual,
      norm_gain, key_cache, value_cache, out_weight, gate_weight, up_weight,
      down_weight)


def solution(mesh):
    S, F, R = mesh.shape["side"], mesh.shape["ffn"], mesh.shape["rep"]
    return jax.shard_map(
        functools.partial(body, S, F, R),
        mesh=mesh,
        in_specs=(
            P(("groups", "side", "rep"), None),
            P(("groups", "side", "rep"), "ffn", None),
            P(("groups", "side", "rep"), "ffn", None),
            P(("groups", "side", "rep"), None),
            P(("groups", "side", "rep"), None),
            P(("groups", "side", "rep")),
            P("groups"),
            P("groups", ("side", "ffn", "rep")),
            P(None, ("side", "ffn", "rep")),
            P(("side", "ffn", "rep")),
            P("rep", ("side", "ffn")),
            P("rep", ("side", "ffn")),
            P("rep", ("side", "ffn")),
        ),
        out_specs=P("groups", ("side", "ffn", "rep")),
        check_vma=False,
    )
```

```python
import functools

import jax
import jax.numpy as jnp
from jax import lax
from jax.experimental import pallas as pl
from jax.experimental.pallas import tpu as pltpu
from jax.sharding import PartitionSpec as P

D = 8192
QUERY_HEADS = 64
KEY_VALUE_HEADS = 8
HEAD_WIDTH = 128
GROUP_WIDTH = QUERY_HEADS // KEY_VALUE_HEADS
OUT_CHUNKS = 4
TURN_COLS = 256
WO_AT = 2
TURNS = ((0, 2), (2, 5), (5, 7))

norm_eps = 1e-05
MESH = pl.DeviceIdType.MESH
NT = (((1,), (1,)), ((), ()))
f32 = jnp.float32
bf16 = jnp.bfloat16


def kernel(
    S, F, R,
    q_hbm, dk_hbm, dv_hbm, len_hbm, cnt_hbm, res_hbm, gain_hbm,
    k_hbm, v_hbm, wo_hbm, wg_hbm, wu_hbm, wd_hbm,
    out_ref,
    q_ref, dk_ref, dv_ref, len_ref, cnt_ref, res_ref, gain_ref,
    k_v, v_v, wo_v, wt_v, wd_v,
    qbd, acc_buf, stat_buf, att_row, att_buf, att_full,
    y_buf,
    sib_send, sib_recv, gu_send, gu_recv, hid, d_send, d_recv,
    small_sem, k_sem, v_sem, wo_sem, raw_sem, wd_sem,
    acc_ss, acc_rs, stat_ss, stat_rs, att_ss, att_rs,
    y_ss, y_rs,
    sib_ss, sib_rs, gu_ss, gu_rs, hid_ss, hid_rs, d_ss, d_rs,
):
    s = lax.axis_index("side")
    f = lax.axis_index("ffn")
    r = lax.axis_index("rep")
    PN = S * F
    SR = S * R
    me = s * F + f
    mine = s * R + r
    rows_q = q_ref.shape[0]
    span = k_v.shape[1]
    total_rows, cols = res_ref.shape
    kv_width = KEY_VALUE_HEADS * HEAD_WIDTH
    unit, seg_cols = wd_v.shape[1:]
    turn = unit % 128 == 0 and seg_cols % 128 == 0
    pair = gu_recv.shape[2] - 128
    up_at = pair // 2
    ahead = PN // 2
    out_rows = wo_v.shape[1]
    scale = HEAD_WIDTH ** (-0.5)

    def dev(side, ffn, rep):
        return {"side": side, "ffn": ffn, "rep": rep}

    def remote(src, dst, ss, rs, to):
        return pltpu.make_async_remote_copy(
            src_ref=src, dst_ref=dst, send_sem=ss, recv_sem=rs, device_id=to, device_id_type=MESH
        )

    def k_copy(i):
        return pltpu.make_async_copy(k_hbm.at[i], k_v.at[i], k_sem.at[i])

    def v_copy(i):
        return pltpu.make_async_copy(v_hbm.at[i], v_v.at[i], v_sem.at[i])

    def wo_copy(i):
        return pltpu.make_async_copy(
            wo_hbm.at[pl.ds(i * out_rows, out_rows)], wo_v.at[i], wo_sem.at[i]
        )

    def unit_rows(p):
        return pl.ds(pl.multiple_of(p * unit, 8), unit)

    def wd_copy(p):
        return pltpu.make_async_copy(wd_hbm.at[unit_rows(p)], wd_v.at[p], wd_sem.at[p])

    def line(j):
        flip = 2 * f // F
        up = j + (j - f + F) // F
        v = F - 1 - j
        down = v - (f - v + F) // F
        last = (j + 1) // F
        return (1 - last) * (flip * up + (1 - flip) * down) + last * f

    def block(own, j):
        side = own * s + (1 - own) * (S - 1 - s)
        ffn = line(j)
        return side, ffn, side * F + ffn

    def in_turn(q):
        last = (q + 1) // PN
        own = (1 - lax.rem(q, 2)) * ((q + PN - 1) // PN) + last
        return block(own, own * (q // 2 - 1 + last) + (1 - own) * ((q + 1) // 2))

    def raw_copy(m, t):
        _, _, p = in_turn(t)
        src = (wg_hbm, wu_hbm)[m].at[unit_rows(p)]
        if turn:
            at = 2 * lax.rem(t, ahead) + m
            return pltpu.make_async_copy(src, wd_v.at[at], raw_sem.at[at])
        return pltpu.make_async_copy(src, wt_v.at[p, pl.ds(m * up_at, unit)], raw_sem.at[2 * t + m])

    def turn_pair(t, c):
        _, _, p = in_turn(t)
        for m in range(2):
            raw_copy(m, t).wait()
            for at in range(0, seg_cols, TURN_COLS):
                wt_v[p, at : at + TURN_COLS, m * up_at : m * up_at + unit] = wd_v[
                    2 * lax.rem(t, ahead) + m, :, at : at + TURN_COLS
                ].T

            @pl.when(t < PN - ahead)
            def _():
                raw_copy(m, t + ahead).start(priority=1)

            @pl.when(t >= PN - ahead)
            def _():
                wd_copy(2 * lax.rem(t, ahead) + m).start(priority=1)

        return c

    def turn_range(lo, hi):
        if turn:
            lax.fori_loop(lo * PN // 8, min(hi * PN // 8, PN - 1), turn_pair, 0)

    def far_first(t):
        last = t // (PN - 2)
        side = (1 - last) * lax.rem(t, 2) + last * (S - 1 - s)
        ffn = line(t // 2)
        return side, ffn, side * F + ffn

    def near_first(t):
        return block(1 - lax.rem(t, 2), F - 1 - t // 2)

    small = [
        pltpu.make_async_copy(src, dst, small_sem.at[n])
        for n, (src, dst) in enumerate((
            (q_hbm, q_ref), (dk_hbm, dk_ref), (dv_hbm, dv_ref), (len_hbm, len_ref),
            (cnt_hbm, cnt_ref), (res_hbm, res_ref), (gain_hbm, gain_ref),
        ))
    ]
    small[0].start()
    k_copy(0).start()
    for copy in small[1:4]:
        copy.start()
    for i in range(1, rows_q):
        k_copy(i).start()
    for i in range(rows_q):
        v_copy(i).start()
    for copy in small[4:]:
        copy.start()
    barrier = pltpu.get_barrier_semaphore()
    group = S * F * R
    my_id = me * R + r

    def greet(t, c):
        other = lax.rem(my_id + t, group)
        pl.semaphore_signal(
            barrier,
            inc=1,
            device_id=dev(other // (F * R), lax.rem(other // R, F), lax.rem(other, R)),
            device_id_type=MESH,
        )
        return c

    lax.fori_loop(1, group, greet, 0)

    qbd[...] = jnp.zeros(qbd.shape, f32)
    for copy in small[:4]:
        copy.wait()
    for i in range(rows_q):
        for h in range(QUERY_HEADS):
            b = h // GROUP_WIDTH
            qbd[i, h : h + 1, b * HEAD_WIDTH : (b + 1) * HEAD_WIDTH] = q_ref[
                i : i + 1, h * HEAD_WIDTH : (h + 1) * HEAD_WIDTH
            ].astype(f32)

    start_pos = f * span
    leading = f == 0
    positions = start_pos + lax.broadcasted_iota(jnp.int32, (QUERY_HEADS, span), 1)
    diag = (
        lax.broadcasted_iota(jnp.int32, (QUERY_HEADS, kv_width), 0) // GROUP_WIDTH
        == lax.broadcasted_iota(jnp.int32, (QUERY_HEADS, kv_width), 1) // HEAD_WIDTH
    )

    def acc_copy(to, slot, i):
        return remote(
            acc_buf.at[slot, i], acc_buf.at[slot, i], acc_ss.at[to, i], acc_rs.at[slot, i],
            dev(s, to, r),
        )

    def stat_copy(to, slot, i):
        return remote(
            stat_buf.at[slot, i], stat_buf.at[slot, i], stat_ss.at[to, i], stat_rs.at[slot, i],
            dev(s, to, r),
        )

    for i in range(rows_q):
        qf = qbd[i]
        fresh = (
            jnp.sum(qf * dk_ref[i : i + 1, :].astype(f32), axis=-1, keepdims=True) * scale
        )
        k_copy(i).wait()
        if i == rows_q - 1:
            def start_gu(t, c):
                raw_copy(0, t).start(priority=1)
                raw_copy(1, t).start(priority=1)
                return c

            lax.fori_loop(0, WO_AT if turn else PN, start_gu, 0)
            for n in range(OUT_CHUNKS):
                wo_copy(n).start(priority=1)
            lax.fori_loop(WO_AT if turn else PN, ahead if turn else PN, start_gu, 0)
        sc = lax.dot_general(qf.astype(bf16), k_v[i], NT, preferred_element_type=f32) * scale
        in_range = positions < len_ref[i]
        peak = jnp.max(jnp.where(in_range, sc, -1e30), axis=-1, keepdims=True)
        peak = jnp.where(leading, jnp.maximum(peak, fresh), peak)
        w = jnp.where(in_range, jnp.exp(sc - peak), 0.0)
        wn = jnp.where(leading, jnp.exp(fresh - peak), 0.0)
        norm = jnp.sum(w, axis=-1, keepdims=True) + wn
        both = jnp.broadcast_to(jnp.concatenate([peak, norm], axis=0), (2 * QUERY_HEADS, 128))
        stat_buf[f, i] = both.T[0:8, :]
        v_copy(i).wait()
        o = jnp.dot(w.astype(bf16), v_v[i], preferred_element_type=f32)
        o = o + wn.astype(bf16).astype(f32) * dv_ref[i : i + 1, :].astype(f32)
        o = jnp.where(diag, o, 0.0)
        part = o[:, :HEAD_WIDTH]
        for b in range(1, KEY_VALUE_HEADS):
            part = part + o[:, b * HEAD_WIDTH : (b + 1) * HEAD_WIDTH]
        acc_buf[f, i] = part.astype(bf16)
        if i == 0:
            pl.semaphore_wait(barrier, group - 1)

        def send_acc(t, c, i=i):
            to = lax.rem(f + t, F)
            stat_copy(to, f, i).start()
            acc_copy(to, f, i).start()
            return c

        lax.fori_loop(1, F, send_acc, 0)

    if not turn:
        def start_down(t, c):
            _, _, p = near_first(t)
            wd_copy(p).start(priority=1)
            return c

        lax.fori_loop(0, PN, start_down, 0)

    turn_range(*TURNS[0])

    def att_copy(other, slot, i):
        return remote(
            att_buf.at[slot, i], att_buf.at[slot, i], att_ss.at[other, i], att_rs.at[slot, i],
            dev(other // R, f, lax.rem(other, R)),
        )

    low = lax.broadcasted_iota(jnp.int32, (8, 128), 1) < QUERY_HEADS
    for i in range(rows_q):
        def recv_acc(t, c, i=i):
            src = lax.rem(f + t, F)
            stat_copy(src, src, i).wait_recv()
            acc_copy(src, src, i).wait_recv()
            return c

        lax.fori_loop(1, F, recv_acc, 0)
        stats = [stat_buf[z, i] for z in range(F)]
        top = stats[0]
        for z in range(1, F):
            top = jnp.maximum(top, stats[z])
        factors = [jnp.exp(v - top) for v in stats]
        total = factors[0] * pltpu.roll(stats[0], QUERY_HEADS, 1)
        for z in range(1, F):
            total = total + factors[z] * pltpu.roll(stats[z], QUERY_HEADS, 1)
        total = jnp.where(low, total, 1.0)
        factors = [v / total for v in factors]
        if 8 * F < 128:
            factors.append(jnp.zeros((128 - 8 * F, 128), f32))
        turned = jnp.concatenate(factors, axis=0).T
        attended = turned[:QUERY_HEADS, 0:1] * acc_buf[0, i].astype(f32)
        for z in range(1, F):
            attended = attended + turned[:QUERY_HEADS, 8 * z : 8 * z + 1] * acc_buf[z, i].astype(f32)
        for h in range(QUERY_HEADS):
            att_row[i : i + 1, h * HEAD_WIDTH : (h + 1) * HEAD_WIDTH] = attended[h : h + 1, :]
        att_buf[mine, i] = att_row[i : i + 1, :].astype(bf16)

        def send_att(t, c, i=i):
            att_copy(lax.rem(mine + t, SR), mine, i).start()
            return c

        lax.fori_loop(1, SR, send_att, 0)

    turn_range(*TURNS[1])

    def recv_att(t, c):
        src = lax.rem(mine + t, SR)
        for i in range(rows_q):
            att_copy(src, src, i).wait_recv()
        return c

    lax.fori_loop(1, SR, recv_att, 0)
    for j in range(SR):
        for i in range(rows_q):
            at = j * rows_q + i
            att_full[at : at + 1, :] = att_buf[j, i].astype(f32)
    for copy in small[4:]:
        copy.wait()
    proj = res_ref[...].astype(f32)
    summed = jnp.zeros((total_rows, cols), f32)
    for i in range(OUT_CHUNKS):
        wo_copy(i).wait()
        summed = summed + jnp.dot(
            att_full[:, i * out_rows : (i + 1) * out_rows].astype(bf16),
            wo_v[i],
            preferred_element_type=f32,
        )
    stream = (proj + summed).astype(bf16).astype(f32)
    lower = lax.broadcasted_iota(jnp.int32, (total_rows, 128), 1) < 64

    def split(v):
        high = v.astype(bf16).astype(f32)
        return jnp.where(lower, high, v - high).astype(bf16)

    def joined(v):
        v = v.astype(f32)
        return v + pltpu.roll(v, 64, 1)

    sq_at = y_buf.shape[2] - 128
    y_buf[r, :, :cols] = (stream * gain_ref[...].astype(f32).reshape(1, cols)).astype(bf16)
    y_buf[r, :, sq_at:] = split(
        jnp.broadcast_to(jnp.sum(stream * stream, axis=1, keepdims=True), (total_rows, 128))
    )

    def y_copy(to, slot):
        return remote(y_buf.at[slot], y_buf.at[slot], y_ss.at[to], y_rs.at[slot], dev(s, f, to))

    def send_y(t, c):
        to = lax.rem(r + t, R)
        y_copy(to, r).start()
        return c

    lax.fori_loop(1, R, send_y, 0)

    aligned = cols % 128 == 0
    turn_range(*TURNS[2])

    def recv_y(t, c):
        src = lax.rem(r + t, R)
        y_copy(src, src).wait_recv()
        return c

    lax.fori_loop(1, R, recv_y, 0)
    squares = joined(y_buf[0, :, sq_at:])
    for j in range(1, R):
        squares = squares + joined(y_buf[j, :, sq_at:])

    def place(j):
        a = lax.broadcasted_iota(jnp.int32, (cols, seg_cols), 0)
        b = lax.broadcasted_iota(jnp.int32, (cols, seg_cols), 1)
        return jnp.where(b == a + j * cols, 1.0, 0.0).astype(bf16)

    if aligned:
        segment = jnp.concatenate([y_buf[j, :, :cols] for j in range(R)], axis=1)
    else:
        segment = jnp.zeros((total_rows, seg_cols), f32)
        for j in range(R):
            segment = segment + jnp.dot(y_buf[j, :, :cols], place(j), preferred_element_type=f32)
        segment = segment.astype(bf16)

    def sib_copy(j):
        ffn = line(j)
        return remote(
            sib_send.at[ffn], sib_recv.at[ffn], sib_ss.at[ffn], sib_rs.at[ffn], dev(S - 1 - s, f, r)
        )

    def gu_copy(ffn, own):
        slot = f if own else ffn
        return remote(
            gu_send.at[ffn], gu_recv.at[slot], gu_ss.at[ffn], gu_rs.at[slot], dev(s, ffn, r)
        )

    def hid_copy(t, own):
        side, ffn, p = far_first(t) if own else near_first(t)
        slot = me if own else p
        return remote(
            hid.at[slot], hid.at[slot], hid_ss.at[p], hid_rs.at[slot], dev(side, ffn, r)
        )

    def project(p):
        if turn:
            return sum(
                jnp.dot(segment[:, at : at + 256], wt_v[p, at : at + 256], preferred_element_type=f32)
                for at in range(0, seg_cols, 256)
            )
        return lax.dot_general(segment, wt_v[p], NT, preferred_element_type=f32)

    def wait_raw(q):
        if not turn:
            raw_copy(0, q).wait()
            raw_copy(1, q).wait()

    def project_sibling(j):
        _, ffn, p = block(0, j)
        sib_send[ffn, :, :pair] = project(p).astype(bf16)
        sib_send[ffn, :, pair:] = split(squares)
        sib_copy(j).start()

    def project_far(j):
        _, ffn, p = block(1, j)
        v = project(p)
        sib_copy(j).wait_recv()
        gu_send[ffn, :, :pair] = (v + sib_recv[ffn, :, :pair].astype(f32)).astype(bf16)
        gu_send[ffn, :, pair:] = split(squares + joined(sib_recv[ffn, :, pair:]))
        gu_copy(ffn, True).start()

    def project_both(j, c):
        wait_raw(2 * j + 1)
        project_sibling(j + 1)
        wait_raw(2 * j + 2)
        project_far(j)
        return c

    wait_raw(0)
    project_sibling(0)
    lax.fori_loop(0, F - 1, project_both, 0)
    if turn:
        sums = []
        for m in range(2):
            at = 2 * lax.rem(PN - 1, ahead) + m
            raw_copy(m, PN - 1).wait()
            sums.append(
                lax.dot_general(segment, wd_v[at], NT, preferred_element_type=f32)
            )
            wd_copy(at).start(priority=1)
        sums = jnp.concatenate(sums, axis=1)
    else:
        wait_raw(PN - 1)
        sums = project(me)
    sib_copy(F - 1).wait_recv()
    sums = sums + sib_recv[f, :, :pair].astype(f32)
    squares = squares + joined(sib_recv[f, :, pair:])

    def gather_sums(t, c):
        src = line(F - 1 - t)
        gu_copy(src, False).wait_recv()
        v = gu_recv[src]
        return c[0] + v[:, :pair].astype(f32), c[1] + joined(v[:, pair:])

    sums, squares = lax.fori_loop(1, F, gather_sums, (sums, squares))
    sums = sums * lax.rsqrt(squares / D + norm_eps)[:, 0:1]
    g = sums[:, :unit]
    u = sums[:, up_at : up_at + unit]
    hid[me] = (g / (1.0 + jnp.exp(-g)) * u).astype(bf16)

    def send_hid(t, c):
        hid_copy(t, True).start()
        return c

    lax.fori_loop(0, PN - 1, send_hid, 0)

    def down(t, c):
        _, _, p = near_first(t)
        wd_copy(p).wait()

        @pl.when(t > 0)
        def _():
            hid_copy(t, False).wait_recv()

        return c + jnp.dot(hid[p], wd_v[p], preferred_element_type=f32)

    terms = jnp.zeros((total_rows, seg_cols), f32)
    terms = lax.fori_loop(0, PN, down, terms, unroll=True)
    terms = terms.astype(bf16)
    for j in range(R):
        if aligned:
            d_send[j] = terms[:, j * cols : (j + 1) * cols]
        else:
            d_send[j] = lax.dot_general(
                terms, place(j), NT, preferred_element_type=f32
            ).astype(bf16)

    def d_copy(to, own):
        return remote(
            d_send.at[to], d_recv.at[r if own else to], d_ss.at[to],
            d_rs.at[r if own else to], dev(s, f, to),
        )

    def send_d(t, c):
        d_copy(lax.rem(r + t, R), True).start()
        return c

    lax.fori_loop(1, R, send_d, 0)

    row = lax.broadcasted_iota(jnp.int32, (total_rows, cols), 0)
    slots = total_rows // cnt_ref.shape[0]
    limit = jnp.zeros((total_rows, cols), jnp.int32)
    for i in range(cnt_ref.shape[0]):
        limit = jnp.where(row // slots == i, cnt_ref[i], limit)
    active = lax.rem(row, slots) < limit

    def recv_d(t, c):
        src = lax.rem(r + t, R)
        d_copy(src, False).wait_recv()
        return c + d_recv[src].astype(f32)

    ffn_out = lax.fori_loop(1, R, recv_d, d_send[r].astype(f32))
    out_ref[...] = jnp.where(active, stream + ffn_out, 0.0).astype(bf16)

    def drain_f(t, c):
        to = lax.rem(f + t, F)
        for i in range(rows_q):
            stat_copy(to, f, i).wait_send()
            acc_copy(to, f, i).wait_send()
        return c

    lax.fori_loop(1, F, drain_f, 0)

    def drain_sr(t, c):
        for i in range(rows_q):
            att_copy(lax.rem(mine + t, SR), mine, i).wait_send()
        return c

    lax.fori_loop(1, SR, drain_sr, 0)

    def drain_r(t, c):
        to = lax.rem(r + t, R)
        y_copy(to, r).wait_send()
        d_copy(to, True).wait_send()
        return c

    lax.fori_loop(1, R, drain_r, 0)

    def drain_p(t, c):
        hid_copy(t, True).wait_send()
        return c

    lax.fori_loop(0, PN - 1, drain_p, 0)

    def drain_sibling(j, c):
        sib_copy(j).wait_send()
        return c

    lax.fori_loop(0, F, drain_sibling, 0)

    def drain_gu(t, c):
        gu_copy(lax.rem(f + t, F), True).wait_send()
        return c

    lax.fori_loop(1, F, drain_gu, 0)


def body(S, F, R, queries, key_cache, value_cache, decoded_key, decoded_value, lengths, counts,
         residual, out_weight, norm_gain, gate_weight, up_weight, down_weight):
    rows_q = queries.shape[0]
    span = key_cache.shape[1]
    kv_width = key_cache.shape[2]
    total_rows, cols = residual.shape
    units, seg_cols = gate_weight.shape
    PN, SR = S * F, S * R
    unit = units // PN
    turn = unit % 128 == 0 and seg_cols % 128 == 0
    pair = 2 * pl.cdiv(unit, 128) * 128
    turned = (seg_cols, pair) if turn else (pair, seg_cols)
    out_rows = out_weight.shape[0] // OUT_CHUNKS
    dma = pltpu.SemaphoreType.DMA
    vmem = pl.BlockSpec(memory_space=pltpu.VMEM)
    hbm = pl.BlockSpec(memory_space=pltpu.HBM)
    return pl.pallas_call(
        functools.partial(kernel, S, F, R),
        out_shape=pltpu.VMEM((total_rows, cols), bf16),
        in_specs=[hbm] * 13,
        out_specs=vmem,
        scratch_shapes=[
            pltpu.VMEM(queries.shape, bf16), pltpu.VMEM(decoded_key.shape, bf16),
            pltpu.VMEM(decoded_value.shape, bf16),
            pltpu.SMEM(lengths.shape, jnp.int32), pltpu.SMEM(counts.shape, jnp.int32),
            pltpu.VMEM(residual.shape, bf16), pltpu.VMEM(norm_gain.shape, bf16),
            pltpu.VMEM((rows_q, span, kv_width), bf16),
            pltpu.VMEM((rows_q, span, kv_width), bf16),
            pltpu.VMEM((OUT_CHUNKS, out_rows, cols), bf16),
            pltpu.VMEM((PN, *turned), bf16),
            pltpu.VMEM((PN, unit, seg_cols), bf16),
            pltpu.VMEM((rows_q, QUERY_HEADS, kv_width), f32),
            pltpu.VMEM((F, rows_q, QUERY_HEADS, HEAD_WIDTH), bf16),
            pltpu.VMEM((F, rows_q, 8, 128), f32),
            pltpu.VMEM((rows_q, QUERY_HEADS * HEAD_WIDTH), f32),
            pltpu.VMEM((SR, rows_q, 1, QUERY_HEADS * HEAD_WIDTH), bf16),
            pltpu.VMEM((total_rows, QUERY_HEADS * HEAD_WIDTH), f32),
            pltpu.VMEM((R, total_rows, pl.cdiv(cols, 128) * 128 + 128), bf16),
            *[pltpu.VMEM((F, total_rows, pair + 128), bf16) for _ in range(4)],
            pltpu.VMEM((PN, total_rows, unit), bf16),
            pltpu.VMEM((R, total_rows, cols), bf16),
            pltpu.VMEM((R, total_rows, cols), bf16),
            dma((7,)), dma((rows_q,)), dma((rows_q,)), dma((OUT_CHUNKS,)),
            dma((2 * PN,)), dma((PN,)),
            dma((F, rows_q)), dma((F, rows_q)), dma((F, rows_q)), dma((F, rows_q)),
            dma((SR, rows_q)), dma((SR, rows_q)),
            dma((R,)), dma((R,)), dma((F,)), dma((F,)), dma((F,)), dma((F,)), dma((PN,)), dma((PN,)),
            dma((R,)), dma((R,)),
        ],
        compiler_params=pltpu.CompilerParams(
            collective_id=0, has_side_effects=True, vmem_limit_bytes=65000000
        ),
        name="decode_step",
    )(queries, decoded_key, decoded_value, lengths, counts, residual,
      norm_gain, key_cache, value_cache, out_weight, gate_weight, up_weight,
      down_weight)


def solution(mesh):
    S, F, R = mesh.shape["side"], mesh.shape["ffn"], mesh.shape["rep"]
    return jax.shard_map(
        functools.partial(body, S, F, R),
        mesh=mesh,
        in_specs=(
            P(("groups", "side", "rep"), None),
            P(("groups", "side", "rep"), "ffn", None),
            P(("groups", "side", "rep"), "ffn", None),
            P(("groups", "side", "rep"), None),
            P(("groups", "side", "rep"), None),
            P(("groups", "side", "rep")),
            P("groups"),
            P("groups", ("side", "ffn", "rep")),
            P(None, ("side", "ffn", "rep")),
            P(("side", "ffn", "rep")),
            P("rep", ("side", "ffn")),
            P("rep", ("side", "ffn")),
            P("rep", ("side", "ffn")),
        ),
        out_specs=P("groups", ("side", "ffn", "rep")),
        check_vma=False,
    )
```

```python
import functools

import jax
import jax.numpy as jnp
from jax import lax
from jax.experimental import pallas as pl
from jax.experimental.pallas import tpu as pltpu
from jax.sharding import PartitionSpec as P

D = 8192
QUERY_HEADS = 64
KEY_VALUE_HEADS = 8
HEAD_WIDTH = 128
GROUP_WIDTH = QUERY_HEADS // KEY_VALUE_HEADS
OUT_CHUNKS = 4
TURN_COLS = 256
WO_AT = 2
TURNS = ((0, 2), (2, 5), (5, 7))

norm_eps = 1e-05
MESH = pl.DeviceIdType.MESH
NT = (((1,), (1,)), ((), ()))
f32 = jnp.float32
bf16 = jnp.bfloat16


def kernel(
    S, F, R,
    q_hbm, dk_hbm, dv_hbm, len_hbm, cnt_hbm, res_hbm, gain_hbm,
    k_hbm, v_hbm, wo_hbm, wg_hbm, wu_hbm, wd_hbm,
    out_ref,
    q_ref, dk_ref, dv_ref, len_ref, cnt_ref, res_ref, gain_ref,
    k_v, v_v, wo_v, wt_v, wd_v,
    q_rows, qbd, acc_buf, stat_buf, att_rows, att_buf, att_full,
    y_buf,
    sib_send, sib_recv, gu_send, gu_recv, hid, d_send, d_recv,
    small_sem, k_sem, v_sem, wo_sem, raw_sem, wd_sem,
    acc_ss, acc_rs, stat_ss, stat_rs, att_ss, att_rs,
    y_ss, y_rs,
    sib_ss, sib_rs, gu_ss, gu_rs, hid_ss, hid_rs, d_ss, d_rs,
):
    s = lax.axis_index("side")
    f = lax.axis_index("ffn")
    r = lax.axis_index("rep")
    PN = S * F
    SR = S * R
    me = s * F + f
    mine = s * R + r
    rows_q = q_ref.shape[0]
    span = k_v.shape[1]
    total_rows, cols = res_ref.shape
    kv_width = KEY_VALUE_HEADS * HEAD_WIDTH
    unit, seg_cols = wd_v.shape[1:]
    turn = unit % 128 == 0 and seg_cols % 128 == 0
    pair = gu_recv.shape[2] - 128
    up_at = pair // 2
    ahead = PN // 2
    out_rows = wo_v.shape[1]
    scale = HEAD_WIDTH ** (-0.5)

    def dev(side, ffn, rep):
        return {"side": side, "ffn": ffn, "rep": rep}

    def remote(src, dst, ss, rs, to):
        return pltpu.make_async_remote_copy(
            src_ref=src, dst_ref=dst, send_sem=ss, recv_sem=rs, device_id=to, device_id_type=MESH
        )

    def k_copy(i):
        return pltpu.make_async_copy(k_hbm.at[i], k_v.at[i], k_sem.at[i])

    def v_copy(i):
        return pltpu.make_async_copy(v_hbm.at[i], v_v.at[i], v_sem.at[i])

    def wo_copy(i):
        return pltpu.make_async_copy(
            wo_hbm.at[pl.ds(i * out_rows, out_rows)], wo_v.at[i], wo_sem.at[i]
        )

    def unit_rows(p):
        return pl.ds(pl.multiple_of(p * unit, 8), unit)

    def wd_copy(p):
        return pltpu.make_async_copy(wd_hbm.at[unit_rows(p)], wd_v.at[p], wd_sem.at[p])

    def line(j):
        flip = 2 * f // F
        up = j + (j - f + F) // F
        v = F - 1 - j
        down = v - (f - v + F) // F
        last = (j + 1) // F
        return (1 - last) * (flip * up + (1 - flip) * down) + last * f

    def block(own, j):
        side = own * s + (1 - own) * (S - 1 - s)
        ffn = line(j)
        return side, ffn, side * F + ffn

    def in_turn(q):
        last = (q + 1) // PN
        own = (1 - lax.rem(q, 2)) * ((q + PN - 1) // PN) + last
        return block(own, own * (q // 2 - 1 + last) + (1 - own) * ((q + 1) // 2))

    def raw_copy(m, t):
        _, _, p = in_turn(t)
        src = (wg_hbm, wu_hbm)[m].at[unit_rows(p)]
        if turn:
            at = 2 * lax.rem(t, ahead) + m
            return pltpu.make_async_copy(src, wd_v.at[at], raw_sem.at[at])
        return pltpu.make_async_copy(src, wt_v.at[p, pl.ds(m * up_at, unit)], raw_sem.at[2 * t + m])

    def turn_pair(t, c):
        _, _, p = in_turn(t)
        for m in range(2):
            raw_copy(m, t).wait()
            for at in range(0, seg_cols, TURN_COLS):
                wt_v[p, at : at + TURN_COLS, m * up_at : m * up_at + unit] = wd_v[
                    2 * lax.rem(t, ahead) + m, :, at : at + TURN_COLS
                ].T

            @pl.when(t < PN - ahead)
            def _():
                raw_copy(m, t + ahead).start(priority=1)

            @pl.when(t >= PN - ahead)
            def _():
                wd_copy(2 * lax.rem(t, ahead) + m).start(priority=1)

        return c

    def turn_range(lo, hi):
        if turn:
            lax.fori_loop(lo * PN // 8, min(hi * PN // 8, PN - 1), turn_pair, 0)

    def far_first(t):
        last = t // (PN - 2)
        side = (1 - last) * lax.rem(t, 2) + last * (S - 1 - s)
        ffn = line(t // 2)
        return side, ffn, side * F + ffn

    def near_first(t):
        return block(1 - lax.rem(t, 2), F - 1 - t // 2)

    small = [
        pltpu.make_async_copy(src, dst, small_sem.at[n])
        for n, (src, dst) in enumerate((
            (q_hbm, q_ref), (dk_hbm, dk_ref), (dv_hbm, dv_ref), (len_hbm, len_ref),
            (cnt_hbm, cnt_ref), (res_hbm, res_ref), (gain_hbm, gain_ref),
        ))
    ]
    small[0].start()
    k_copy(0).start()
    for copy in small[1:4]:
        copy.start()
    for i in range(1, rows_q):
        k_copy(i).start()
    for i in range(rows_q):
        v_copy(i).start()
    for copy in small[4:]:
        copy.start()
    barrier = pltpu.get_barrier_semaphore()
    group = S * F * R
    my_id = me * R + r

    def greet(t, c):
        other = lax.rem(my_id + t, group)
        pl.semaphore_signal(
            barrier,
            inc=1,
            device_id=dev(other // (F * R), lax.rem(other // R, F), lax.rem(other, R)),
            device_id_type=MESH,
        )
        return c

    lax.fori_loop(1, group, greet, 0)

    qbd[...] = jnp.zeros(qbd.shape, bf16)
    for copy in small[:4]:
        copy.wait()
    for h in range(QUERY_HEADS):
        pair_of = q_ref[:, h * HEAD_WIDTH : (h + 1) * HEAD_WIDTH].astype(f32)
        for i in range(rows_q):
            q_rows[i, h : h + 1, :] = pair_of[i : i + 1, :]

    start_pos = f * span
    leading = f == 0
    positions = start_pos + lax.broadcasted_iota(jnp.int32, (1, span), 1)
    heads = [
        (slice(b * GROUP_WIDTH, (b + 1) * GROUP_WIDTH), slice(b * HEAD_WIDTH, (b + 1) * HEAD_WIDTH))
        for b in range(KEY_VALUE_HEADS)
    ]
    for i in range(rows_q):
        for at, lanes in heads:
            qbd[i, at, lanes] = q_rows[i, at, :].astype(bf16)

    def acc_copy(to, slot, i):
        return remote(
            acc_buf.at[slot, i], acc_buf.at[slot, i], acc_ss.at[to, i], acc_rs.at[slot, i],
            dev(s, to, r),
        )

    def stat_copy(to, slot, i):
        return remote(
            stat_buf.at[slot, i], stat_buf.at[slot, i], stat_ss.at[to, i], stat_rs.at[slot, i],
            dev(s, to, r),
        )

    for i in range(rows_q):
        fresh = scale * jnp.concatenate(
            [
                jnp.sum(q_rows[i, at, :] * dk_ref[i : i + 1, lanes].astype(f32), axis=-1, keepdims=True)
                for at, lanes in heads
            ],
            axis=0,
        )
        k_copy(i).wait()
        if i == rows_q - 1:
            def start_gu(t, c):
                raw_copy(0, t).start(priority=1)
                raw_copy(1, t).start(priority=1)
                return c

            lax.fori_loop(0, WO_AT if turn else PN, start_gu, 0)
            for n in range(OUT_CHUNKS):
                wo_copy(n).start(priority=1)
            lax.fori_loop(WO_AT if turn else PN, ahead if turn else PN, start_gu, 0)
        sc = lax.dot_general(qbd[i], k_v[i], NT, preferred_element_type=f32) * scale
        sc = sc + jnp.where(positions < len_ref[i], 0.0, -1e30)
        peak = jnp.maximum(jnp.max(sc, axis=-1, keepdims=True), -1e29)
        peak = jnp.where(leading, jnp.maximum(peak, fresh), peak)
        w = jnp.exp(sc - peak)
        wn = jnp.where(leading, jnp.exp(fresh - peak), 0.0)
        norm = jnp.sum(w, axis=-1, keepdims=True) + wn
        both = jnp.broadcast_to(jnp.concatenate([peak, norm], axis=0), (2 * QUERY_HEADS, 128))
        stat_buf[f, i] = both.T[0:8, :]
        v_copy(i).wait()
        o = jnp.dot(w.astype(bf16), v_v[i], preferred_element_type=f32)
        wn = wn.astype(bf16).astype(f32)
        acc_buf[f, i] = jnp.concatenate(
            [o[at, lanes] + wn[at] * dv_ref[i : i + 1, lanes].astype(f32) for at, lanes in heads],
            axis=0,
        ).astype(bf16)
        if i == 0:
            pl.semaphore_wait(barrier, group - 1)

        def send_acc(t, c, i=i):
            to = lax.rem(f + t, F)
            stat_copy(to, f, i).start()
            acc_copy(to, f, i).start()
            return c

        lax.fori_loop(1, F, send_acc, 0)

    if not turn:
        def start_down(t, c):
            _, _, p = near_first(t)
            wd_copy(p).start(priority=1)
            return c

        lax.fori_loop(0, PN, start_down, 0)

    turn_range(*TURNS[0])

    def att_copy(other, slot, i):
        return remote(
            att_buf.at[slot, i], att_buf.at[slot, i], att_ss.at[other, i], att_rs.at[slot, i],
            dev(other // R, f, lax.rem(other, R)),
        )

    low = lax.broadcasted_iota(jnp.int32, (8, 128), 1) < QUERY_HEADS
    for i in range(rows_q):
        def recv_acc(t, c, i=i):
            src = lax.rem(f + t, F)
            stat_copy(src, src, i).wait_recv()
            acc_copy(src, src, i).wait_recv()
            return c

        lax.fori_loop(1, F, recv_acc, 0)
        stats = [stat_buf[z, i] for z in range(F)]
        top = stats[0]
        for z in range(1, F):
            top = jnp.maximum(top, stats[z])
        factors = [jnp.exp(v - top) for v in stats]
        total = factors[0] * pltpu.roll(stats[0], QUERY_HEADS, 1)
        for z in range(1, F):
            total = total + factors[z] * pltpu.roll(stats[z], QUERY_HEADS, 1)
        total = jnp.where(low, total, 1.0)
        factors = [v / total for v in factors]
        if 8 * F < 128:
            factors.append(jnp.zeros((128 - 8 * F, 128), f32))
        turned = jnp.concatenate(factors, axis=0).T
        attended = turned[:QUERY_HEADS, 0:1] * acc_buf[0, i].astype(f32)
        for z in range(1, F):
            attended = attended + turned[:QUERY_HEADS, 8 * z : 8 * z + 1] * acc_buf[z, i].astype(f32)
        att_rows[...] = attended
        att_buf[mine, i] = jnp.concatenate(
            [att_rows[h : h + 1, :] for h in range(QUERY_HEADS)], axis=1
        ).astype(bf16)

        def send_att(t, c, i=i):
            att_copy(lax.rem(mine + t, SR), mine, i).start()
            return c

        lax.fori_loop(1, SR, send_att, 0)

    turn_range(*TURNS[1])

    for t in range(SR):
        src = lax.rem(mine + t * R + t * R // SR, SR)
        for i in range(rows_q):
            if t > 0:
                att_copy(src, src, i).wait_recv()
            att_full[pl.ds(src * rows_q + i, 1), :] = att_buf[src, i].astype(f32)
    for copy in small[4:]:
        copy.wait()
    proj = res_ref[...].astype(f32)
    summed = jnp.zeros((total_rows, cols), f32)
    for i in range(OUT_CHUNKS):
        wo_copy(i).wait()
        summed = summed + jnp.dot(
            att_full[:, i * out_rows : (i + 1) * out_rows].astype(bf16),
            wo_v[i],
            preferred_element_type=f32,
        )
    stream = (proj + summed).astype(bf16).astype(f32)
    lower = lax.broadcasted_iota(jnp.int32, (total_rows, 128), 1) < 64

    def split(v):
        high = v.astype(bf16).astype(f32)
        return jnp.where(lower, high, v - high).astype(bf16)

    def joined(v):
        v = v.astype(f32)
        return v + pltpu.roll(v, 64, 1)

    sq_at = y_buf.shape[2] - 128
    y_buf[r, :, :cols] = (stream * gain_ref[...].astype(f32).reshape(1, cols)).astype(bf16)
    y_buf[r, :, sq_at:] = split(
        jnp.broadcast_to(jnp.sum(stream * stream, axis=1, keepdims=True), (total_rows, 128))
    )

    def y_copy(to, slot):
        return remote(y_buf.at[slot], y_buf.at[slot], y_ss.at[to], y_rs.at[slot], dev(s, f, to))

    def send_y(t, c):
        to = lax.rem(r + t, R)
        y_copy(to, r).start()
        return c

    lax.fori_loop(1, R, send_y, 0)

    aligned = cols % 128 == 0
    turn_range(*TURNS[2])

    def recv_y(t, c):
        src = lax.rem(r + t, R)
        y_copy(src, src).wait_recv()
        return c

    lax.fori_loop(1, R, recv_y, 0)
    squares = joined(y_buf[0, :, sq_at:])
    for j in range(1, R):
        squares = squares + joined(y_buf[j, :, sq_at:])

    def place(j):
        a = lax.broadcasted_iota(jnp.int32, (cols, seg_cols), 0)
        b = lax.broadcasted_iota(jnp.int32, (cols, seg_cols), 1)
        return jnp.where(b == a + j * cols, 1.0, 0.0).astype(bf16)

    if aligned:
        segment = jnp.concatenate([y_buf[j, :, :cols] for j in range(R)], axis=1)
    else:
        segment = jnp.zeros((total_rows, seg_cols), f32)
        for j in range(R):
            segment = segment + jnp.dot(y_buf[j, :, :cols], place(j), preferred_element_type=f32)
        segment = segment.astype(bf16)

    def sib_copy(j):
        ffn = line(j)
        return remote(
            sib_send.at[ffn], sib_recv.at[ffn], sib_ss.at[ffn], sib_rs.at[ffn], dev(S - 1 - s, f, r)
        )

    def gu_copy(ffn, own):
        slot = f if own else ffn
        return remote(
            gu_send.at[ffn], gu_recv.at[slot], gu_ss.at[ffn], gu_rs.at[slot], dev(s, ffn, r)
        )

    def hid_copy(t, own):
        side, ffn, p = far_first(t) if own else near_first(t)
        slot = me if own else p
        return remote(
            hid.at[slot], hid.at[slot], hid_ss.at[p], hid_rs.at[slot], dev(side, ffn, r)
        )

    def project(p):
        if turn:
            return sum(
                jnp.dot(segment[:, at : at + 256], wt_v[p, at : at + 256], preferred_element_type=f32)
                for at in range(0, seg_cols, 256)
            )
        return lax.dot_general(segment, wt_v[p], NT, preferred_element_type=f32)

    def wait_raw(q):
        if not turn:
            raw_copy(0, q).wait()
            raw_copy(1, q).wait()

    def project_sibling(j):
        _, ffn, p = block(0, j)
        sib_send[ffn, :, :pair] = project(p).astype(bf16)
        sib_send[ffn, :, pair:] = split(squares)
        sib_copy(j).start()

    def project_far(j, ffn, v):
        sib_copy(j).wait_recv()
        gu_send[ffn, :, :pair] = (v + sib_recv[ffn, :, :pair].astype(f32)).astype(bf16)
        gu_send[ffn, :, pair:] = split(squares + joined(sib_recv[ffn, :, pair:]))
        gu_copy(ffn, True).start()

    def project_both(j, c):
        wait_raw(2 * j + 1)
        wait_raw(2 * j + 2)
        _, sib, p = block(0, j + 1)
        _, ffn, q = block(1, j)
        a = project(p)
        v = project(q)
        sib_send[sib, :, :pair] = a.astype(bf16)
        sib_send[sib, :, pair:] = split(squares)
        sib_copy(j + 1).start()
        project_far(j, ffn, v)
        return c

    wait_raw(0)
    project_sibling(0)
    lax.fori_loop(0, F - 1, project_both, 0)
    if turn:
        sums = []
        for m in range(2):
            at = 2 * lax.rem(PN - 1, ahead) + m
            raw_copy(m, PN - 1).wait()
            sums.append(
                lax.dot_general(segment, wd_v[at], NT, preferred_element_type=f32)
            )
            wd_copy(at).start(priority=1)
        sums = jnp.concatenate(sums, axis=1)
    else:
        wait_raw(PN - 1)
        sums = project(me)
    sib_copy(F - 1).wait_recv()
    sums = sums + sib_recv[f, :, :pair].astype(f32)
    squares = squares + joined(sib_recv[f, :, pair:])

    def gather_sums(t, c):
        src = line(F - 1 - t)
        gu_copy(src, False).wait_recv()
        v = gu_recv[src]
        return c[0] + v[:, :pair].astype(f32), c[1] + joined(v[:, pair:])

    sums, squares = lax.fori_loop(1, F, gather_sums, (sums, squares))
    sums = sums * lax.rsqrt(squares / D + norm_eps)[:, 0:1]
    g = sums[:, :unit]
    u = sums[:, up_at : up_at + unit]
    hid[me] = (g / (1.0 + jnp.exp(-g)) * u).astype(bf16)

    def send_hid(t, c):
        hid_copy(t, True).start()
        return c

    lax.fori_loop(0, PN - 1, send_hid, 0)

    def down(t, c):
        _, _, p = near_first(t)
        wd_copy(p).wait()

        @pl.when(t > 0)
        def _():
            hid_copy(t, False).wait_recv()

        return c + jnp.dot(hid[p], wd_v[p], preferred_element_type=f32)

    terms = jnp.zeros((total_rows, seg_cols), f32)
    terms = lax.fori_loop(0, PN, down, terms, unroll=True)
    terms = terms.astype(bf16)
    for j in range(R):
        if aligned:
            d_send[j] = terms[:, j * cols : (j + 1) * cols]
        else:
            d_send[j] = lax.dot_general(
                terms, place(j), NT, preferred_element_type=f32
            ).astype(bf16)

    def d_copy(to, own):
        return remote(
            d_send.at[to], d_recv.at[r if own else to], d_ss.at[to],
            d_rs.at[r if own else to], dev(s, f, to),
        )

    def send_d(t, c):
        d_copy(lax.rem(r + t, R), True).start()
        return c

    lax.fori_loop(1, R, send_d, 0)

    row = lax.broadcasted_iota(jnp.int32, (total_rows, cols), 0)
    slots = total_rows // cnt_ref.shape[0]
    limit = jnp.zeros((total_rows, cols), jnp.int32)
    for i in range(cnt_ref.shape[0]):
        limit = jnp.where(row // slots == i, cnt_ref[i], limit)
    active = lax.rem(row, slots) < limit

    def recv_d(t, c):
        src = lax.rem(r + t, R)
        d_copy(src, False).wait_recv()
        return c + d_recv[src].astype(f32)

    ffn_out = lax.fori_loop(1, R, recv_d, d_send[r].astype(f32))
    out_ref[...] = jnp.where(active, stream + ffn_out, 0.0).astype(bf16)

    def drain_f(t, c):
        to = lax.rem(f + t, F)
        for i in range(rows_q):
            stat_copy(to, f, i).wait_send()
            acc_copy(to, f, i).wait_send()
        return c

    lax.fori_loop(1, F, drain_f, 0)

    def drain_sr(t, c):
        for i in range(rows_q):
            att_copy(lax.rem(mine + t, SR), mine, i).wait_send()
        return c

    lax.fori_loop(1, SR, drain_sr, 0)

    def drain_r(t, c):
        to = lax.rem(r + t, R)
        y_copy(to, r).wait_send()
        d_copy(to, True).wait_send()
        return c

    lax.fori_loop(1, R, drain_r, 0)

    def drain_p(t, c):
        hid_copy(t, True).wait_send()
        return c

    lax.fori_loop(0, PN - 1, drain_p, 0)

    def drain_sibling(j, c):
        sib_copy(j).wait_send()
        return c

    lax.fori_loop(0, F, drain_sibling, 0)

    def drain_gu(t, c):
        gu_copy(lax.rem(f + t, F), True).wait_send()
        return c

    lax.fori_loop(1, F, drain_gu, 0)


def body(S, F, R, queries, key_cache, value_cache, decoded_key, decoded_value, lengths, counts,
         residual, out_weight, norm_gain, gate_weight, up_weight, down_weight):
    rows_q = queries.shape[0]
    span = key_cache.shape[1]
    kv_width = key_cache.shape[2]
    total_rows, cols = residual.shape
    units, seg_cols = gate_weight.shape
    PN, SR = S * F, S * R
    unit = units // PN
    turn = unit % 128 == 0 and seg_cols % 128 == 0
    pair = 2 * pl.cdiv(unit, 128) * 128
    turned = (seg_cols, pair) if turn else (pair, seg_cols)
    out_rows = out_weight.shape[0] // OUT_CHUNKS
    dma = pltpu.SemaphoreType.DMA
    vmem = pl.BlockSpec(memory_space=pltpu.VMEM)
    hbm = pl.BlockSpec(memory_space=pltpu.HBM)
    return pl.pallas_call(
        functools.partial(kernel, S, F, R),
        out_shape=pltpu.VMEM((total_rows, cols), bf16),
        in_specs=[hbm] * 13,
        out_specs=vmem,
        scratch_shapes=[
            pltpu.VMEM(queries.shape, bf16), pltpu.VMEM(decoded_key.shape, bf16),
            pltpu.VMEM(decoded_value.shape, bf16),
            pltpu.SMEM(lengths.shape, jnp.int32), pltpu.SMEM(counts.shape, jnp.int32),
            pltpu.VMEM(residual.shape, bf16), pltpu.VMEM(norm_gain.shape, bf16),
            pltpu.VMEM((rows_q, span, kv_width), bf16),
            pltpu.VMEM((rows_q, span, kv_width), bf16),
            pltpu.VMEM((OUT_CHUNKS, out_rows, cols), bf16),
            pltpu.VMEM((PN, *turned), bf16),
            pltpu.VMEM((PN, unit, seg_cols), bf16),
            pltpu.VMEM((rows_q, QUERY_HEADS, HEAD_WIDTH), f32),
            pltpu.VMEM((rows_q, QUERY_HEADS, kv_width), bf16),
            pltpu.VMEM((F, rows_q, QUERY_HEADS, HEAD_WIDTH), bf16),
            pltpu.VMEM((F, rows_q, 8, 128), f32),
            pltpu.VMEM((QUERY_HEADS, HEAD_WIDTH), f32),
            pltpu.VMEM((SR, rows_q, 1, QUERY_HEADS * HEAD_WIDTH), bf16),
            pltpu.VMEM((total_rows, QUERY_HEADS * HEAD_WIDTH), f32),
            pltpu.VMEM((R, total_rows, pl.cdiv(cols, 128) * 128 + 128), bf16),
            *[pltpu.VMEM((F, total_rows, pair + 128), bf16) for _ in range(4)],
            pltpu.VMEM((PN, total_rows, unit), bf16),
            pltpu.VMEM((R, total_rows, cols), bf16),
            pltpu.VMEM((R, total_rows, cols), bf16),
            dma((7,)), dma((rows_q,)), dma((rows_q,)), dma((OUT_CHUNKS,)),
            dma((2 * PN,)), dma((PN,)),
            dma((F, rows_q)), dma((F, rows_q)), dma((F, rows_q)), dma((F, rows_q)),
            dma((SR, rows_q)), dma((SR, rows_q)),
            dma((R,)), dma((R,)), dma((F,)), dma((F,)), dma((F,)), dma((F,)), dma((PN,)), dma((PN,)),
            dma((R,)), dma((R,)),
        ],
        compiler_params=pltpu.CompilerParams(
            collective_id=0, has_side_effects=True, vmem_limit_bytes=65000000
        ),
        name="decode_step",
    )(queries, decoded_key, decoded_value, lengths, counts, residual,
      norm_gain, key_cache, value_cache, out_weight, gate_weight, up_weight,
      down_weight)


def solution(mesh):
    S, F, R = mesh.shape["side"], mesh.shape["ffn"], mesh.shape["rep"]
    return jax.shard_map(
        functools.partial(body, S, F, R),
        mesh=mesh,
        in_specs=(
            P(("groups", "side", "rep"), None),
            P(("groups", "side", "rep"), "ffn", None),
            P(("groups", "side", "rep"), "ffn", None),
            P(("groups", "side", "rep"), None),
            P(("groups", "side", "rep"), None),
            P(("groups", "side", "rep")),
            P("groups"),
            P("groups", ("side", "ffn", "rep")),
            P(None, ("side", "ffn", "rep")),
            P(("side", "ffn", "rep")),
            P("rep", ("side", "ffn")),
            P("rep", ("side", "ffn")),
            P("rep", ("side", "ffn")),
        ),
        out_specs=P("groups", ("side", "ffn", "rep")),
        check_vma=False,
    )
```

```python
import functools

import jax
import jax.numpy as jnp
from jax import lax
from jax.experimental import pallas as pl
from jax.experimental.pallas import tpu as pltpu
from jax.sharding import PartitionSpec as P

D = 8192
QUERY_HEADS = 64
KEY_VALUE_HEADS = 8
HEAD_WIDTH = 128
GROUP_WIDTH = QUERY_HEADS // KEY_VALUE_HEADS
OUT_CHUNKS = 4
TURN_COLS = 256
WO_AT = 2
TURNS = ((0, 2), (2, 5), (5, 7))

norm_eps = 1e-05
MESH = pl.DeviceIdType.MESH
NT = (((1,), (1,)), ((), ()))
f32 = jnp.float32
bf16 = jnp.bfloat16


def kernel(
    S, F, R,
    q_hbm, dk_hbm, dv_hbm, len_hbm, cnt_hbm, res_hbm, gain_hbm,
    k_hbm, v_hbm, wo_hbm, wg_hbm, wu_hbm, wd_hbm,
    out_ref,
    q_ref, dk_ref, dv_ref, len_ref, cnt_ref, res_ref, gain_ref,
    k_v, v_v, wo_v, wt_v, wd_v,
    q_rows, qbd, acc_buf, stat_buf, att_rows, att_buf, att_full,
    y_buf,
    sib_send, sib_recv, gu_send, gu_recv, hid, d_send, d_recv,
    small_sem, k_sem, v_sem, wo_sem, raw_sem, wd_sem,
    acc_ss, acc_rs, stat_ss, stat_rs, att_ss, att_rs,
    y_ss, y_rs,
    sib_ss, sib_rs, gu_ss, gu_rs, hid_ss, hid_rs, d_ss, d_rs,
):
    s = lax.axis_index("side")
    f = lax.axis_index("ffn")
    r = lax.axis_index("rep")
    PN = S * F
    SR = S * R
    me = s * F + f
    mine = s * R + r
    rows_q = q_ref.shape[0]
    span = k_v.shape[1]
    total_rows, cols = res_ref.shape
    kv_width = KEY_VALUE_HEADS * HEAD_WIDTH
    unit, seg_cols = wd_v.shape[1:]
    turn = unit % 128 == 0 and seg_cols % 128 == 0
    pair = gu_recv.shape[2] - 128
    up_at = pair // 2
    ahead = PN // 2
    out_rows = wo_v.shape[1]
    scale = HEAD_WIDTH ** (-0.5)

    def dev(side, ffn, rep):
        return {"side": side, "ffn": ffn, "rep": rep}

    def remote(src, dst, ss, rs, to):
        return pltpu.make_async_remote_copy(
            src_ref=src, dst_ref=dst, send_sem=ss, recv_sem=rs, device_id=to, device_id_type=MESH
        )

    def k_copy(i):
        return pltpu.make_async_copy(k_hbm.at[i], k_v.at[i], k_sem.at[i])

    def v_copy(i):
        return pltpu.make_async_copy(v_hbm.at[i], v_v.at[i], v_sem.at[i])

    def wo_copy(i):
        return pltpu.make_async_copy(
            wo_hbm.at[pl.ds(i * out_rows, out_rows)], wo_v.at[i], wo_sem.at[i]
        )

    def unit_rows(p):
        return pl.ds(pl.multiple_of(p * unit, 8), unit)

    def wd_copy(p):
        return pltpu.make_async_copy(wd_hbm.at[unit_rows(p)], wd_v.at[p], wd_sem.at[p])

    flip = lax.div(2 * f, F)

    def line(j):
        v = F - 1 - j
        up = j + lax.div(j - f + F, F)
        down = v - lax.div(f - v + F, F)
        if isinstance(j, int):
            return f if j == F - 1 else flip * up + (1 - flip) * down
        last = lax.div(j + 1, F)
        return (1 - last) * (flip * up + (1 - flip) * down) + last * f

    lines = [line(j) for j in range(F)]

    def block(own, j):
        side = own * s + (1 - own) * (S - 1 - s)
        ffn = line(j)
        return side, ffn, side * F + ffn

    def in_turn(q):
        last = lax.div(q + 1, PN)
        own = (1 - lax.rem(q, 2)) * lax.div(q + PN - 1, PN) + last
        half = lax.div(q, 2)
        return block(own, own * (half - 1 + last) + (1 - own) * (half + lax.rem(q, 2)))

    def raw_copy(m, t):
        _, _, p = in_turn(t)
        src = (wg_hbm, wu_hbm)[m].at[unit_rows(p)]
        if turn:
            at = 2 * lax.rem(t, ahead) + m
            return pltpu.make_async_copy(src, wd_v.at[at], raw_sem.at[at])
        return pltpu.make_async_copy(src, wt_v.at[p, pl.ds(m * up_at, unit)], raw_sem.at[2 * t + m])

    def turn_pair(t, c):
        _, _, p = in_turn(t)
        for m in range(2):
            raw_copy(m, t).wait()
            for at in range(0, seg_cols, TURN_COLS):
                wt_v[p, at : at + TURN_COLS, m * up_at : m * up_at + unit] = wd_v[
                    2 * lax.rem(t, ahead) + m, :, at : at + TURN_COLS
                ].T

            @pl.when(t < PN - ahead)
            def _():
                raw_copy(m, t + ahead).start(priority=1)

            @pl.when(t >= PN - ahead)
            def _():
                wd_copy(2 * lax.rem(t, ahead) + m).start(priority=1)

        return c

    def turn_range(lo, hi):
        if turn:
            lax.fori_loop(lo * PN // 8, min(hi * PN // 8, PN - 1), turn_pair, 0)

    def far_first(t):
        side = S - 1 - s if t == PN - 2 else t % 2
        ffn = lines[t // 2]
        return side, ffn, side * F + ffn

    def near_first(t):
        side = s if t % 2 == 0 else S - 1 - s
        ffn = lines[F - 1 - t // 2]
        return side, ffn, side * F + ffn

    small = [
        pltpu.make_async_copy(src, dst, small_sem.at[n])
        for n, (src, dst) in enumerate((
            (q_hbm, q_ref), (dk_hbm, dk_ref), (dv_hbm, dv_ref), (len_hbm, len_ref),
            (cnt_hbm, cnt_ref), (res_hbm, res_ref), (gain_hbm, gain_ref),
        ))
    ]
    small[0].start()
    k_copy(0).start()
    for copy in small[1:4]:
        copy.start()
    for i in range(1, rows_q):
        k_copy(i).start()
    for i in range(rows_q):
        v_copy(i).start()
    for copy in small[4:]:
        copy.start()
    barrier = pltpu.get_barrier_semaphore()
    group = S * F * R
    my_id = me * R + r

    def greet(t, c):
        other = lax.rem(my_id + t, group)
        pl.semaphore_signal(
            barrier,
            inc=1,
            device_id=dev(other // (F * R), lax.rem(other // R, F), lax.rem(other, R)),
            device_id_type=MESH,
        )
        return c

    lax.fori_loop(1, group, greet, 0)

    qbd[...] = jnp.zeros(qbd.shape, bf16)
    for copy in small[:4]:
        copy.wait()
    for h in range(QUERY_HEADS):
        pair_of = q_ref[:, h * HEAD_WIDTH : (h + 1) * HEAD_WIDTH].astype(f32)
        for i in range(rows_q):
            q_rows[i, h : h + 1, :] = pair_of[i : i + 1, :]

    start_pos = f * span
    leading = f == 0
    positions = start_pos + lax.broadcasted_iota(jnp.int32, (1, span), 1)
    heads = [
        (slice(b * GROUP_WIDTH, (b + 1) * GROUP_WIDTH), slice(b * HEAD_WIDTH, (b + 1) * HEAD_WIDTH))
        for b in range(KEY_VALUE_HEADS)
    ]
    for i in range(rows_q):
        for at, lanes in heads:
            qbd[i, at, lanes] = q_rows[i, at, :].astype(bf16)

    def acc_copy(to, slot, i):
        return remote(
            acc_buf.at[slot, i], acc_buf.at[slot, i], acc_ss.at[to, i], acc_rs.at[slot, i],
            dev(s, to, r),
        )

    def stat_copy(to, slot, i):
        return remote(
            stat_buf.at[slot, i], stat_buf.at[slot, i], stat_ss.at[to, i], stat_rs.at[slot, i],
            dev(s, to, r),
        )

    for i in range(rows_q):
        fresh = scale * jnp.concatenate(
            [
                jnp.sum(q_rows[i, at, :] * dk_ref[i : i + 1, lanes].astype(f32), axis=-1, keepdims=True)
                for at, lanes in heads
            ],
            axis=0,
        )
        k_copy(i).wait()
        if i == rows_q - 1:
            def start_gu(t, c):
                raw_copy(0, t).start(priority=1)
                raw_copy(1, t).start(priority=1)
                return c

            lax.fori_loop(0, WO_AT if turn else PN, start_gu, 0)
            for n in range(OUT_CHUNKS):
                wo_copy(n).start(priority=1)
            lax.fori_loop(WO_AT if turn else PN, ahead if turn else PN, start_gu, 0)
        sc = lax.dot_general(qbd[i], k_v[i], NT, preferred_element_type=f32) * scale
        sc = sc + jnp.where(positions < len_ref[i], 0.0, -1e30)
        peak = jnp.maximum(jnp.max(sc, axis=-1, keepdims=True), -1e29)
        peak = jnp.where(leading, jnp.maximum(peak, fresh), peak)
        w = jnp.exp(sc - peak)
        wn = jnp.where(leading, jnp.exp(fresh - peak), 0.0)
        norm = jnp.sum(w, axis=-1, keepdims=True) + wn
        both = jnp.broadcast_to(jnp.concatenate([peak, norm], axis=0), (2 * QUERY_HEADS, 128))
        stat_buf[f, i] = both.T[0:8, :]
        v_copy(i).wait()
        o = jnp.dot(w.astype(bf16), v_v[i], preferred_element_type=f32)
        wn = wn.astype(bf16).astype(f32)
        acc_buf[f, i] = jnp.concatenate(
            [o[at, lanes] + wn[at] * dv_ref[i : i + 1, lanes].astype(f32) for at, lanes in heads],
            axis=0,
        ).astype(bf16)
        if i == 0:
            pl.semaphore_wait(barrier, group - 1)

        def send_acc(t, c, i=i):
            to = lax.rem(f + t, F)
            stat_copy(to, f, i).start()
            acc_copy(to, f, i).start()
            return c

        lax.fori_loop(1, F, send_acc, 0)

    if not turn:
        for t in range(PN):
            wd_copy(near_first(t)[2]).start(priority=1)

    turn_range(*TURNS[0])

    def att_copy(other, slot, i):
        return remote(
            att_buf.at[slot, i], att_buf.at[slot, i], att_ss.at[other, i], att_rs.at[slot, i],
            dev(other // R, f, lax.rem(other, R)),
        )

    low = lax.broadcasted_iota(jnp.int32, (8, 128), 1) < QUERY_HEADS
    for i in range(rows_q):
        def recv_acc(t, c, i=i):
            src = lax.rem(f + t, F)
            stat_copy(src, src, i).wait_recv()
            acc_copy(src, src, i).wait_recv()
            return c

        lax.fori_loop(1, F, recv_acc, 0)
        stats = [stat_buf[z, i] for z in range(F)]
        top = stats[0]
        for z in range(1, F):
            top = jnp.maximum(top, stats[z])
        factors = [jnp.exp(v - top) for v in stats]
        total = factors[0] * pltpu.roll(stats[0], QUERY_HEADS, 1)
        for z in range(1, F):
            total = total + factors[z] * pltpu.roll(stats[z], QUERY_HEADS, 1)
        total = jnp.where(low, total, 1.0)
        factors = [v / total for v in factors]
        if 8 * F < 128:
            factors.append(jnp.zeros((128 - 8 * F, 128), f32))
        turned = jnp.concatenate(factors, axis=0).T
        attended = turned[:QUERY_HEADS, 0:1] * acc_buf[0, i].astype(f32)
        for z in range(1, F):
            attended = attended + turned[:QUERY_HEADS, 8 * z : 8 * z + 1] * acc_buf[z, i].astype(f32)
        att_rows[...] = attended
        att_buf[mine, i] = jnp.concatenate(
            [att_rows[h : h + 1, :] for h in range(QUERY_HEADS)], axis=1
        ).astype(bf16)

        def send_att(t, c, i=i):
            att_copy(lax.rem(mine + t, SR), mine, i).start()
            return c

        lax.fori_loop(1, SR, send_att, 0)

    turn_range(*TURNS[1])

    for i in range(OUT_CHUNKS):
        wo_copy(i).wait()
    for t in range(SR):
        src = lax.rem(mine + t * R + t * R // SR, SR)
        for i in range(rows_q):
            if t > 0:
                att_copy(src, src, i).wait_recv()
            att_full[pl.ds(src * rows_q + i, 1), :] = att_buf[src, i].astype(f32)
    for copy in small[4:]:
        copy.wait()
    proj = res_ref[...].astype(f32)
    summed = jnp.zeros((total_rows, cols), f32)
    for i in range(OUT_CHUNKS):
        summed = summed + jnp.dot(
            att_full[:, i * out_rows : (i + 1) * out_rows].astype(bf16),
            wo_v[i],
            preferred_element_type=f32,
        )
    stream = (proj + summed).astype(bf16).astype(f32)
    lower = lax.broadcasted_iota(jnp.int32, (total_rows, 128), 1) < 64

    def split(v):
        high = v.astype(bf16).astype(f32)
        return jnp.where(lower, high, v - high).astype(bf16)

    def joined(v):
        v = v.astype(f32)
        return v + pltpu.roll(v, 64, 1)

    sq_at = y_buf.shape[2] - 128
    y_buf[r, :, :cols] = (stream * gain_ref[...].astype(f32).reshape(1, cols)).astype(bf16)
    y_buf[r, :, sq_at:] = split(
        jnp.broadcast_to(jnp.sum(stream * stream, axis=1, keepdims=True), (total_rows, 128))
    )

    def y_copy(to, slot):
        return remote(y_buf.at[slot], y_buf.at[slot], y_ss.at[to], y_rs.at[slot], dev(s, f, to))

    def send_y(t, c):
        to = lax.rem(r + t, R)
        y_copy(to, r).start()
        return c

    lax.fori_loop(1, R, send_y, 0)

    aligned = cols % 128 == 0
    turn_range(*TURNS[2])

    def recv_y(t, c):
        src = lax.rem(r + t, R)
        y_copy(src, src).wait_recv()
        return c

    lax.fori_loop(1, R, recv_y, 0)
    squares = joined(y_buf[0, :, sq_at:])
    for j in range(1, R):
        squares = squares + joined(y_buf[j, :, sq_at:])

    def place(j):
        a = lax.broadcasted_iota(jnp.int32, (cols, seg_cols), 0)
        b = lax.broadcasted_iota(jnp.int32, (cols, seg_cols), 1)
        return jnp.where(b == a + j * cols, 1.0, 0.0).astype(bf16)

    if aligned:
        segment = jnp.concatenate([y_buf[j, :, :cols] for j in range(R)], axis=1)
    else:
        segment = jnp.zeros((total_rows, seg_cols), f32)
        for j in range(R):
            segment = segment + jnp.dot(y_buf[j, :, :cols], place(j), preferred_element_type=f32)
        segment = segment.astype(bf16)

    def sib_copy(j):
        ffn = line(j)
        return remote(
            sib_send.at[ffn], sib_recv.at[ffn], sib_ss.at[ffn], sib_rs.at[ffn], dev(S - 1 - s, f, r)
        )

    def gu_copy(ffn, own):
        slot = f if own else ffn
        return remote(
            gu_send.at[ffn], gu_recv.at[slot], gu_ss.at[ffn], gu_rs.at[slot], dev(s, ffn, r)
        )

    def hid_copy(t, own):
        side, ffn, p = far_first(t) if own else near_first(t)
        slot = me if own else p
        return remote(
            hid.at[slot], hid.at[slot], hid_ss.at[p], hid_rs.at[slot], dev(side, ffn, r)
        )

    def project(p):
        if turn:
            return sum(
                jnp.dot(segment[:, at : at + 256], wt_v[p, at : at + 256], preferred_element_type=f32)
                for at in range(0, seg_cols, 256)
            )
        return lax.dot_general(segment, wt_v[p], NT, preferred_element_type=f32)

    def wait_raw(q):
        if not turn:
            raw_copy(0, q).wait()
            raw_copy(1, q).wait()

    def project_sibling(j):
        _, ffn, p = block(0, j)
        sib_send[ffn, :, :pair] = project(p).astype(bf16)
        sib_send[ffn, :, pair:] = split(squares)
        sib_copy(j).start()

    def project_far(j, ffn, v):
        sib_copy(j).wait_recv()
        gu_send[ffn, :, :pair] = (v + sib_recv[ffn, :, :pair].astype(f32)).astype(bf16)
        gu_send[ffn, :, pair:] = split(squares + joined(sib_recv[ffn, :, pair:]))
        gu_copy(ffn, True).start()

    def project_both(j, c):
        wait_raw(2 * j + 1)
        wait_raw(2 * j + 2)
        _, sib, p = block(0, j + 1)
        _, ffn, q = block(1, j)
        a = project(p)
        v = project(q)
        sib_send[sib, :, :pair] = a.astype(bf16)
        sib_send[sib, :, pair:] = split(squares)
        sib_copy(j + 1).start()
        project_far(j, ffn, v)
        return c

    wait_raw(0)
    project_sibling(0)
    lax.fori_loop(0, F - 1, project_both, 0)
    if turn:
        sums = []
        for m in range(2):
            at = 2 * lax.rem(PN - 1, ahead) + m
            raw_copy(m, PN - 1).wait()
            sums.append(
                lax.dot_general(segment, wd_v[at], NT, preferred_element_type=f32)
            )
            wd_copy(at).start(priority=1)
        sums = jnp.concatenate(sums, axis=1)
    else:
        wait_raw(PN - 1)
        sums = project(me)
    sib_copy(F - 1).wait_recv()
    sums = sums + sib_recv[f, :, :pair].astype(f32)
    squares = squares + joined(sib_recv[f, :, pair:])

    for t in range(1, F):
        src = lines[F - 1 - t]
        gu_copy(src, False).wait_recv()
        v = gu_recv[src]
        sums = sums + v[:, :pair].astype(f32)
        squares = squares + joined(v[:, pair:])

    sums = sums * lax.rsqrt(squares / D + norm_eps)[:, 0:1]
    g = sums[:, :unit]
    u = sums[:, up_at : up_at + unit]
    hid[me] = (g / (1.0 + jnp.exp(-g)) * u).astype(bf16)

    for t in range(PN - 1):
        hid_copy(t, True).start()

    def drain_f(t, c):
        to = lax.rem(f + t, F)
        for i in range(rows_q):
            stat_copy(to, f, i).wait_send()
            acc_copy(to, f, i).wait_send()
        gu_copy(to, True).wait_send()
        return c

    lax.fori_loop(1, F, drain_f, 0)

    def drain_sr(t, c):
        for i in range(rows_q):
            att_copy(lax.rem(mine + t, SR), mine, i).wait_send()
        return c

    lax.fori_loop(1, SR, drain_sr, 0)

    def drain_y(t, c):
        y_copy(lax.rem(r + t, R), r).wait_send()
        return c

    lax.fori_loop(1, R, drain_y, 0)

    for j in range(F):
        sib_copy(j).wait_send()

    terms = jnp.zeros((total_rows, seg_cols), f32)
    for t in range(PN):
        p = near_first(t)[2]
        wd_copy(p).wait()
        if t > 0:
            hid_copy(t, False).wait_recv()
        terms = terms + jnp.dot(hid[p], wd_v[p], preferred_element_type=f32)
    terms = terms.astype(bf16)
    for j in range(R):
        if aligned:
            d_send[j] = terms[:, j * cols : (j + 1) * cols]
        else:
            d_send[j] = lax.dot_general(
                terms, place(j), NT, preferred_element_type=f32
            ).astype(bf16)

    def d_copy(to, own):
        return remote(
            d_send.at[to], d_recv.at[r if own else to], d_ss.at[to],
            d_rs.at[r if own else to], dev(s, f, to),
        )

    def send_d(t, c):
        d_copy(lax.rem(r + t, R), True).start()
        return c

    lax.fori_loop(1, R, send_d, 0)

    row = lax.broadcasted_iota(jnp.int32, (total_rows, cols), 0)
    slots = total_rows // cnt_ref.shape[0]
    limit = jnp.zeros((total_rows, cols), jnp.int32)
    for i in range(cnt_ref.shape[0]):
        limit = jnp.where(row // slots == i, cnt_ref[i], limit)
    active = lax.rem(row, slots) < limit

    for t in range(PN - 1):
        hid_copy(t, True).wait_send()

    def recv_d(t, c):
        src = lax.rem(r + t, R)
        d_copy(src, False).wait_recv()
        return c + d_recv[src].astype(f32)

    ffn_out = lax.fori_loop(1, R, recv_d, d_send[r].astype(f32))
    out_ref[...] = jnp.where(active, stream + ffn_out, 0.0).astype(bf16)

    def drain_d(t, c):
        d_copy(lax.rem(r + t, R), True).wait_send()
        return c

    lax.fori_loop(1, R, drain_d, 0)


def body(S, F, R, queries, key_cache, value_cache, decoded_key, decoded_value, lengths, counts,
         residual, out_weight, norm_gain, gate_weight, up_weight, down_weight):
    rows_q = queries.shape[0]
    span = key_cache.shape[1]
    kv_width = key_cache.shape[2]
    total_rows, cols = residual.shape
    units, seg_cols = gate_weight.shape
    PN, SR = S * F, S * R
    unit = units // PN
    turn = unit % 128 == 0 and seg_cols % 128 == 0
    pair = 2 * pl.cdiv(unit, 128) * 128
    turned = (seg_cols, pair) if turn else (pair, seg_cols)
    out_rows = out_weight.shape[0] // OUT_CHUNKS
    dma = pltpu.SemaphoreType.DMA
    vmem = pl.BlockSpec(memory_space=pltpu.VMEM)
    hbm = pl.BlockSpec(memory_space=pltpu.HBM)
    return pl.pallas_call(
        functools.partial(kernel, S, F, R),
        out_shape=pltpu.VMEM((total_rows, cols), bf16),
        in_specs=[hbm] * 13,
        out_specs=vmem,
        scratch_shapes=[
            pltpu.VMEM(queries.shape, bf16), pltpu.VMEM(decoded_key.shape, bf16),
            pltpu.VMEM(decoded_value.shape, bf16),
            pltpu.SMEM(lengths.shape, jnp.int32), pltpu.SMEM(counts.shape, jnp.int32),
            pltpu.VMEM(residual.shape, bf16), pltpu.VMEM(norm_gain.shape, bf16),
            pltpu.VMEM((rows_q, span, kv_width), bf16),
            pltpu.VMEM((rows_q, span, kv_width), bf16),
            pltpu.VMEM((OUT_CHUNKS, out_rows, cols), bf16),
            pltpu.VMEM((PN, *turned), bf16),
            pltpu.VMEM((PN, unit, seg_cols), bf16),
            pltpu.VMEM((rows_q, QUERY_HEADS, HEAD_WIDTH), f32),
            pltpu.VMEM((rows_q, QUERY_HEADS, kv_width), bf16),
            pltpu.VMEM((F, rows_q, QUERY_HEADS, HEAD_WIDTH), bf16),
            pltpu.VMEM((F, rows_q, 8, 128), f32),
            pltpu.VMEM((QUERY_HEADS, HEAD_WIDTH), f32),
            pltpu.VMEM((SR, rows_q, 1, QUERY_HEADS * HEAD_WIDTH), bf16),
            pltpu.VMEM((total_rows, QUERY_HEADS * HEAD_WIDTH), f32),
            pltpu.VMEM((R, total_rows, pl.cdiv(cols, 128) * 128 + 128), bf16),
            *[pltpu.VMEM((F, total_rows, pair + 128), bf16) for _ in range(4)],
            pltpu.VMEM((PN, total_rows, unit), bf16),
            pltpu.VMEM((R, total_rows, cols), bf16),
            pltpu.VMEM((R, total_rows, cols), bf16),
            dma((7,)), dma((rows_q,)), dma((rows_q,)), dma((OUT_CHUNKS,)),
            dma((2 * PN,)), dma((PN,)),
            dma((F, rows_q)), dma((F, rows_q)), dma((F, rows_q)), dma((F, rows_q)),
            dma((SR, rows_q)), dma((SR, rows_q)),
            dma((R,)), dma((R,)), dma((F,)), dma((F,)), dma((F,)), dma((F,)), dma((PN,)), dma((PN,)),
            dma((R,)), dma((R,)),
        ],
        compiler_params=pltpu.CompilerParams(
            collective_id=0, has_side_effects=True, vmem_limit_bytes=65000000
        ),
        name="decode_step",
    )(queries, decoded_key, decoded_value, lengths, counts, residual,
      norm_gain, key_cache, value_cache, out_weight, gate_weight, up_weight,
      down_weight)


def solution(mesh):
    S, F, R = mesh.shape["side"], mesh.shape["ffn"], mesh.shape["rep"]
    return jax.shard_map(
        functools.partial(body, S, F, R),
        mesh=mesh,
        in_specs=(
            P(("groups", "side", "rep"), None),
            P(("groups", "side", "rep"), "ffn", None),
            P(("groups", "side", "rep"), "ffn", None),
            P(("groups", "side", "rep"), None),
            P(("groups", "side", "rep"), None),
            P(("groups", "side", "rep")),
            P("groups"),
            P("groups", ("side", "ffn", "rep")),
            P(None, ("side", "ffn", "rep")),
            P(("side", "ffn", "rep")),
            P("rep", ("side", "ffn")),
            P("rep", ("side", "ffn")),
            P("rep", ("side", "ffn")),
        ),
        out_specs=P("groups", ("side", "ffn", "rep")),
        check_vma=False,
    )
```

```python
import functools

import jax
import jax.numpy as jnp
from jax import lax
from jax.experimental import pallas as pl
from jax.experimental.pallas import tpu as pltpu
from jax.sharding import PartitionSpec as P

D = 8192
QUERY_HEADS = 64
KEY_VALUE_HEADS = 8
HEAD_WIDTH = 128
GROUP_WIDTH = QUERY_HEADS // KEY_VALUE_HEADS
OUT_CHUNKS = 4
TURN_COLS = 256
WO_AT = 2
TURNS = ((0, 2), (2, 4), (4, 6))

norm_eps = 1e-05
MESH = pl.DeviceIdType.MESH
NT = (((1,), (1,)), ((), ()))
f32 = jnp.float32
bf16 = jnp.bfloat16


def kernel(
    S, F, R,
    q_hbm, dk_hbm, dv_hbm, len_hbm, cnt_hbm, res_hbm, gain_hbm,
    k_hbm, v_hbm, wo_hbm, wg_hbm, wu_hbm, wd_hbm,
    out_ref,
    q_ref, dk_ref, dv_ref, len_ref, cnt_ref, res_ref, gain_ref,
    k_v, v_v, wo_v, wt_v, wd_v,
    q_rows, qbd, acc_buf, stat_buf, att_rows, att_buf, att_full,
    y_buf,
    sib_send, sib_recv, gu_send, gu_recv, hid, d_send, d_recv,
    small_sem, k_sem, v_sem, wo_sem, raw_sem, wd_sem,
    acc_ss, acc_rs, stat_ss, stat_rs, att_ss, att_rs,
    y_ss, y_rs,
    sib_ss, sib_rs, gu_ss, gu_rs, hid_ss, hid_rs, d_ss, d_rs,
):
    s = lax.axis_index("side")
    f = lax.axis_index("ffn")
    r = lax.axis_index("rep")
    PN = S * F
    SR = S * R
    me = s * F + f
    mine = s * R + r
    rows_q = q_ref.shape[0]
    span = k_v.shape[1]
    total_rows, cols = res_ref.shape
    kv_width = KEY_VALUE_HEADS * HEAD_WIDTH
    unit, seg_cols = wd_v.shape[1:]
    turn = unit % 128 == 0 and seg_cols % 128 == 0
    pair = gu_recv.shape[2] - 128
    up_at = pair // 2
    ahead = PN // 2
    out_rows = wo_v.shape[1]
    scale = HEAD_WIDTH ** (-0.5)

    def dev(side, ffn, rep):
        return {"side": side, "ffn": ffn, "rep": rep}

    def remote(src, dst, ss, rs, to):
        return pltpu.make_async_remote_copy(
            src_ref=src, dst_ref=dst, send_sem=ss, recv_sem=rs, device_id=to, device_id_type=MESH
        )

    def k_copy(i):
        return pltpu.make_async_copy(k_hbm.at[i], k_v.at[i], k_sem.at[i])

    def v_copy(i):
        return pltpu.make_async_copy(v_hbm.at[i], v_v.at[i], v_sem.at[i])

    def wo_copy(i):
        return pltpu.make_async_copy(
            wo_hbm.at[pl.ds(i * out_rows, out_rows)], wo_v.at[i], wo_sem.at[i]
        )

    def unit_rows(p):
        return pl.ds(pl.multiple_of(p * unit, 8), unit)

    def wd_copy(p):
        return pltpu.make_async_copy(wd_hbm.at[unit_rows(p)], wd_v.at[p], wd_sem.at[p])

    flip = lax.div(2 * f, F)

    def line(j):
        v = F - 1 - j
        up = j + lax.div(j - f + F, F)
        down = v - lax.div(f - v + F, F)
        if isinstance(j, int):
            return f if j == F - 1 else flip * up + (1 - flip) * down
        last = lax.div(j + 1, F)
        return (1 - last) * (flip * up + (1 - flip) * down) + last * f

    lines = [line(j) for j in range(F)]

    def block(own, j):
        side = own * s + (1 - own) * (S - 1 - s)
        ffn = line(j)
        return side, ffn, side * F + ffn

    def in_turn(q):
        q = q + lax.div(q + 3, PN) - 2 * lax.div(q + 2, PN) + lax.div(q + 1, PN)
        last = lax.div(q + 1, PN)
        own = (1 - lax.rem(q, 2)) * lax.div(q + PN - 1, PN) + last
        half = lax.div(q, 2)
        return block(own, own * (half - 1 + last) + (1 - own) * (half + lax.rem(q, 2)))

    def raw_copy(m, t):
        _, _, p = in_turn(t)
        src = (wg_hbm, wu_hbm)[m].at[unit_rows(p)]
        if turn:
            at = 2 * lax.rem(t, ahead) + m
            return pltpu.make_async_copy(src, wd_v.at[at], raw_sem.at[at])
        return pltpu.make_async_copy(src, wt_v.at[p, pl.ds(m * up_at, unit)], raw_sem.at[2 * t + m])

    def turn_pair(t, c):
        _, _, p = in_turn(t)
        for m in range(2):
            raw_copy(m, t).wait()
            for at in range(0, seg_cols, TURN_COLS):
                wt_v[p, at : at + TURN_COLS, m * up_at : m * up_at + unit] = wd_v[
                    2 * lax.rem(t, ahead) + m, :, at : at + TURN_COLS
                ].T

            @pl.when(t < PN - ahead)
            def _():
                raw_copy(m, t + ahead).start(priority=1)

            @pl.when(t >= PN - ahead)
            def _():
                wd_copy(2 * lax.rem(t, ahead) + m).start(priority=1)

        return c

    def turn_range(lo, hi):
        if turn:
            lax.fori_loop(lo * PN // 8, min(hi * PN // 8, PN - 2), turn_pair, 0)

    def far_first(t):
        side = S - 1 - s if t == PN - 2 else t % 2
        ffn = lines[t // 2]
        return side, ffn, side * F + ffn

    def near_first(t):
        side = s if t % 2 == 0 else S - 1 - s
        ffn = lines[F - 1 - t // 2]
        return side, ffn, side * F + ffn

    small = [
        pltpu.make_async_copy(src, dst, small_sem.at[n])
        for n, (src, dst) in enumerate((
            (q_hbm, q_ref), (dk_hbm, dk_ref), (dv_hbm, dv_ref), (len_hbm, len_ref),
            (cnt_hbm, cnt_ref), (res_hbm, res_ref), (gain_hbm, gain_ref),
        ))
    ]
    small[0].start()
    k_copy(0).start()
    for copy in small[1:4]:
        copy.start()
    v_copy(0).start()
    for i in range(1, rows_q):
        k_copy(i).start()
        v_copy(i).start()
    for copy in small[4:]:
        copy.start()
    barrier = pltpu.get_barrier_semaphore()
    group = S * F * R
    my_id = me * R + r

    def greet(t, c):
        other = lax.rem(my_id + t, group)
        pl.semaphore_signal(
            barrier,
            inc=1,
            device_id=dev(lax.div(other, F * R), lax.rem(lax.div(other, R), F), lax.rem(other, R)),
            device_id_type=MESH,
        )
        return c

    lax.fori_loop(1, group, greet, 0)

    qbd[...] = jnp.zeros(qbd.shape, bf16)
    for copy in small[:4]:
        copy.wait()
    for h in range(QUERY_HEADS):
        pair_of = q_ref[:, h * HEAD_WIDTH : (h + 1) * HEAD_WIDTH].astype(f32)
        for i in range(rows_q):
            q_rows[i, h : h + 1, :] = pair_of[i : i + 1, :]

    start_pos = f * span
    leading = f == 0
    positions = start_pos + lax.broadcasted_iota(jnp.int32, (1, span), 1)
    heads = [
        (slice(b * GROUP_WIDTH, (b + 1) * GROUP_WIDTH), slice(b * HEAD_WIDTH, (b + 1) * HEAD_WIDTH))
        for b in range(KEY_VALUE_HEADS)
    ]
    for i in range(rows_q):
        for at, lanes in heads:
            qbd[i, at, lanes] = q_rows[i, at, :].astype(bf16)

    def acc_copy(to, slot, i):
        return remote(
            acc_buf.at[slot, i], acc_buf.at[slot, i], acc_ss.at[to, i], acc_rs.at[slot, i],
            dev(s, to, r),
        )

    def stat_copy(to, slot, i):
        return remote(
            stat_buf.at[slot, i], stat_buf.at[slot, i], stat_ss.at[to, i], stat_rs.at[slot, i],
            dev(s, to, r),
        )

    for i in range(rows_q):
        fresh = scale * jnp.concatenate(
            [
                jnp.sum(q_rows[i, at, :] * dk_ref[i : i + 1, lanes].astype(f32), axis=-1, keepdims=True)
                for at, lanes in heads
            ],
            axis=0,
        )
        k_copy(i).wait()
        if i == rows_q - 1:
            def start_gu(t, c):
                raw_copy(0, t).start(priority=1)
                raw_copy(1, t).start(priority=1)
                return c

            lax.fori_loop(0, WO_AT if turn else PN, start_gu, 0)
            for n in range(OUT_CHUNKS):
                wo_copy(n).start(priority=1)
            lax.fori_loop(WO_AT if turn else PN, ahead if turn else PN, start_gu, 0)
        sc = lax.dot_general(qbd[i], k_v[i], NT, preferred_element_type=f32) * scale
        sc = sc + jnp.where(positions < len_ref[i], 0.0, -1e30)
        peak = jnp.maximum(jnp.max(sc, axis=-1, keepdims=True), -1e29)
        peak = jnp.where(leading, jnp.maximum(peak, fresh), peak)
        w = jnp.exp(sc - peak)
        wn = jnp.where(leading, jnp.exp(fresh - peak), 0.0)
        norm = jnp.sum(w, axis=-1, keepdims=True) + wn
        both = jnp.broadcast_to(jnp.concatenate([peak, norm], axis=0), (2 * QUERY_HEADS, 128))
        stat_buf[f, i] = both.T[0:8, :]
        v_copy(i).wait()
        o = jnp.dot(w.astype(bf16), v_v[i], preferred_element_type=f32)
        wn = wn.astype(bf16).astype(f32)
        acc_buf[f, i] = jnp.concatenate(
            [o[at, lanes] + wn[at] * dv_ref[i : i + 1, lanes].astype(f32) for at, lanes in heads],
            axis=0,
        ).astype(bf16)
        if i == 0:
            pl.semaphore_wait(barrier, group - 1)

        def send_acc(t, c, i=i):
            to = lax.rem(f + t, F)
            stat_copy(to, f, i).start()
            acc_copy(to, f, i).start()
            return c

        lax.fori_loop(1, F, send_acc, 0)

    if not turn:
        for t in range(PN):
            wd_copy(near_first(t)[2]).start(priority=1)

    turn_range(*TURNS[0])

    def att_copy(other, slot, i):
        return remote(
            att_buf.at[slot, i], att_buf.at[slot, i], att_ss.at[other, i], att_rs.at[slot, i],
            dev(lax.div(other, R), f, lax.rem(other, R)),
        )

    low = lax.broadcasted_iota(jnp.int32, (8, 128), 1) < QUERY_HEADS
    for i in range(rows_q):
        def recv_acc(t, c, i=i):
            src = lax.rem(f + t, F)
            stat_copy(src, src, i).wait_recv()
            acc_copy(src, src, i).wait_recv()
            return c

        lax.fori_loop(1, F, recv_acc, 0)
        stats = [stat_buf[z, i] for z in range(F)]
        top = stats[0]
        for z in range(1, F):
            top = jnp.maximum(top, stats[z])
        factors = [jnp.exp(v - top) for v in stats]
        total = factors[0] * pltpu.roll(stats[0], QUERY_HEADS, 1)
        for z in range(1, F):
            total = total + factors[z] * pltpu.roll(stats[z], QUERY_HEADS, 1)
        total = jnp.where(low, total, 1.0)
        factors = [v / total for v in factors]
        if 8 * F < 128:
            factors.append(jnp.zeros((128 - 8 * F, 128), f32))
        turned = jnp.concatenate(factors, axis=0).T
        attended = turned[:QUERY_HEADS, 0:1] * acc_buf[0, i].astype(f32)
        for z in range(1, F):
            attended = attended + turned[:QUERY_HEADS, 8 * z : 8 * z + 1] * acc_buf[z, i].astype(f32)
        att_rows[...] = attended
        att_buf[mine, i] = jnp.concatenate(
            [att_rows[h : h + 1, :] for h in range(QUERY_HEADS)], axis=1
        ).astype(bf16)

        def send_att(t, c, i=i):
            att_copy(lax.rem(mine + t, SR), mine, i).start()
            return c

        lax.fori_loop(1, SR, send_att, 0)

    turn_range(*TURNS[1])

    for i in range(OUT_CHUNKS):
        wo_copy(i).wait()
    for t in range(SR):
        src = lax.rem(mine + t * R + t * R // SR, SR)
        for i in range(rows_q):
            if t > 0:
                att_copy(src, src, i).wait_recv()
            att_full[pl.ds(src * rows_q + i, 1), :] = att_buf[src, i].astype(f32)
    for copy in small[4:]:
        copy.wait()
    proj = res_ref[...].astype(f32)
    summed = jnp.zeros((total_rows, cols), f32)
    for i in range(OUT_CHUNKS):
        summed = summed + jnp.dot(
            att_full[:, i * out_rows : (i + 1) * out_rows].astype(bf16),
            wo_v[i],
            preferred_element_type=f32,
        )
    stream = (proj + summed).astype(bf16).astype(f32)
    lower = lax.broadcasted_iota(jnp.int32, (total_rows, 128), 1) < 64

    def split(v):
        high = v.astype(bf16).astype(f32)
        return jnp.where(lower, high, v - high).astype(bf16)

    def joined(v):
        v = v.astype(f32)
        return v + pltpu.roll(v, 64, 1)

    sq_at = y_buf.shape[2] - 128
    y_buf[r, :, :cols] = (stream * gain_ref[...].astype(f32).reshape(1, cols)).astype(bf16)
    y_buf[r, :, sq_at:] = split(
        jnp.broadcast_to(jnp.sum(stream * stream, axis=1, keepdims=True), (total_rows, 128))
    )

    def y_copy(to, slot):
        return remote(y_buf.at[slot], y_buf.at[slot], y_ss.at[to], y_rs.at[slot], dev(s, f, to))

    def send_y(t, c):
        to = lax.rem(r + t, R)
        y_copy(to, r).start()
        return c

    lax.fori_loop(1, R, send_y, 0)

    aligned = cols % 128 == 0
    turn_range(*TURNS[2])

    def recv_y(t, c):
        src = lax.rem(r + t, R)
        y_copy(src, src).wait_recv()
        return c

    lax.fori_loop(1, R, recv_y, 0)
    squares = joined(y_buf[0, :, sq_at:])
    for j in range(1, R):
        squares = squares + joined(y_buf[j, :, sq_at:])

    def place(j):
        a = lax.broadcasted_iota(jnp.int32, (cols, seg_cols), 0)
        b = lax.broadcasted_iota(jnp.int32, (cols, seg_cols), 1)
        return jnp.where(b == a + j * cols, 1.0, 0.0).astype(bf16)

    if aligned:
        segment = jnp.concatenate([y_buf[j, :, :cols] for j in range(R)], axis=1)
    else:
        segment = jnp.zeros((total_rows, seg_cols), f32)
        for j in range(R):
            segment = segment + jnp.dot(y_buf[j, :, :cols], place(j), preferred_element_type=f32)
        segment = segment.astype(bf16)

    def sib_copy(j):
        ffn = line(j)
        return remote(
            sib_send.at[ffn], sib_recv.at[ffn], sib_ss.at[ffn], sib_rs.at[ffn], dev(S - 1 - s, f, r)
        )

    def gu_copy(ffn, own):
        slot = f if own else ffn
        return remote(
            gu_send.at[ffn], gu_recv.at[slot], gu_ss.at[ffn], gu_rs.at[slot], dev(s, ffn, r)
        )

    def hid_copy(t, own):
        side, ffn, p = far_first(t) if own else near_first(t)
        slot = me if own else p
        return remote(
            hid.at[slot], hid.at[slot], hid_ss.at[p], hid_rs.at[slot], dev(side, ffn, r)
        )

    def project(p):
        if turn:
            return sum(
                jnp.dot(segment[:, at : at + 256], wt_v[p, at : at + 256], preferred_element_type=f32)
                for at in range(0, seg_cols, 256)
            )
        return lax.dot_general(segment, wt_v[p], NT, preferred_element_type=f32)

    def wait_raw(q):
        if not turn:
            raw_copy(0, q).wait()
            raw_copy(1, q).wait()

    def project_stored(q, p):
        if not turn:
            wait_raw(q)
            return project(p)
        both = []
        for m in range(2):
            at = 2 * (q % ahead) + m
            raw_copy(m, q).wait()
            both.append(lax.dot_general(segment, wd_v[at], NT, preferred_element_type=f32))
        for m in range(2):
            wd_copy(2 * (q % ahead) + m).start(priority=1)
        return jnp.concatenate(both, axis=1)

    def send_sibling(j, v):
        ffn = lines[j]
        sib_send[ffn, :, :pair] = v.astype(bf16)
        sib_send[ffn, :, pair:] = split(squares)
        sib_copy(j).start()

    def project_far(j, ffn, v):
        sib_copy(j).wait_recv()
        gu_send[ffn, :, :pair] = (v + sib_recv[ffn, :, :pair].astype(f32)).astype(bf16)
        gu_send[ffn, :, pair:] = split(squares + joined(sib_recv[ffn, :, pair:]))
        gu_copy(ffn, True).start()

    def project_both(j, c):
        wait_raw(2 * j + 1)
        wait_raw(2 * j + 2)
        _, sib, p = block(0, j + 1)
        _, ffn, q = block(1, j)
        a = project(p)
        v = project(q)
        sib_send[sib, :, :pair] = a.astype(bf16)
        sib_send[sib, :, pair:] = split(squares)
        sib_copy(j + 1).start()
        project_far(j, ffn, v)
        return c

    wait_raw(0)
    send_sibling(0, project(block(0, 0)[2]))
    lax.fori_loop(0, F - 2, project_both, 0)
    wait_raw(PN - 3)
    _, near, at_near = block(1, F - 2)
    project_far(F - 2, near, project(at_near))
    send_sibling(F - 1, project_stored(PN - 2, block(0, F - 1)[2]))
    sums = project_stored(PN - 1, me)
    sib_copy(F - 1).wait_recv()
    sums = sums + sib_recv[f, :, :pair].astype(f32)
    squares = squares + joined(sib_recv[f, :, pair:])

    for t in range(1, F):
        src = lines[F - 1 - t]
        gu_copy(src, False).wait_recv()
        v = gu_recv[src]
        sums = sums + v[:, :pair].astype(f32)
        squares = squares + joined(v[:, pair:])

    sums = sums * lax.rsqrt(squares / D + norm_eps)[:, 0:1]
    g = sums[:, :unit]
    u = sums[:, up_at : up_at + unit]
    hid[me] = (g / (1.0 + jnp.exp(-g)) * u).astype(bf16)

    for t in range(PN - 1):
        hid_copy(t, True).start()

    def drain_f(t, c):
        to = lax.rem(f + t, F)
        for i in range(rows_q):
            stat_copy(to, f, i).wait_send()
            acc_copy(to, f, i).wait_send()
        gu_copy(to, True).wait_send()
        return c

    lax.fori_loop(1, F, drain_f, 0)

    def drain_sr(t, c):
        for i in range(rows_q):
            att_copy(lax.rem(mine + t, SR), mine, i).wait_send()
        return c

    lax.fori_loop(1, SR, drain_sr, 0)

    def drain_y(t, c):
        y_copy(lax.rem(r + t, R), r).wait_send()
        return c

    lax.fori_loop(1, R, drain_y, 0)

    for j in range(F):
        sib_copy(j).wait_send()

    terms = jnp.zeros((total_rows, seg_cols), f32)
    for t in range(PN):
        p = near_first(t)[2]
        wd_copy(p).wait()
        if t > 0:
            hid_copy(t, False).wait_recv()
        terms = terms + jnp.dot(hid[p], wd_v[p], preferred_element_type=f32)
    terms = terms.astype(bf16)
    for j in range(R):
        if aligned:
            d_send[j] = terms[:, j * cols : (j + 1) * cols]
        else:
            d_send[j] = lax.dot_general(
                terms, place(j), NT, preferred_element_type=f32
            ).astype(bf16)

    def d_copy(to, own):
        return remote(
            d_send.at[to], d_recv.at[r if own else to], d_ss.at[to],
            d_rs.at[r if own else to], dev(s, f, to),
        )

    def send_d(t, c):
        d_copy(lax.rem(r + t, R), True).start()
        return c

    lax.fori_loop(1, R, send_d, 0)

    row = lax.broadcasted_iota(jnp.int32, (total_rows, cols), 0)
    slots = total_rows // cnt_ref.shape[0]
    limit = jnp.zeros((total_rows, cols), jnp.int32)
    for i in range(cnt_ref.shape[0]):
        limit = jnp.where(row // slots == i, cnt_ref[i], limit)
    active = lax.rem(row, slots) < limit

    for t in range(PN - 1):
        hid_copy(t, True).wait_send()

    def recv_d(t, c):
        src = lax.rem(r + t, R)
        d_copy(src, False).wait_recv()
        return c + d_recv[src].astype(f32)

    ffn_out = lax.fori_loop(1, R, recv_d, d_send[r].astype(f32))
    out_ref[...] = jnp.where(active, stream + ffn_out, 0.0).astype(bf16)

    def drain_d(t, c):
        d_copy(lax.rem(r + t, R), True).wait_send()
        return c

    lax.fori_loop(1, R, drain_d, 0)


def body(S, F, R, queries, key_cache, value_cache, decoded_key, decoded_value, lengths, counts,
         residual, out_weight, norm_gain, gate_weight, up_weight, down_weight):
    rows_q = queries.shape[0]
    span = key_cache.shape[1]
    kv_width = key_cache.shape[2]
    total_rows, cols = residual.shape
    units, seg_cols = gate_weight.shape
    PN, SR = S * F, S * R
    unit = units // PN
    turn = unit % 128 == 0 and seg_cols % 128 == 0
    pair = 2 * pl.cdiv(unit, 128) * 128
    turned = (seg_cols, pair) if turn else (pair, seg_cols)
    out_rows = out_weight.shape[0] // OUT_CHUNKS
    dma = pltpu.SemaphoreType.DMA
    vmem = pl.BlockSpec(memory_space=pltpu.VMEM)
    hbm = pl.BlockSpec(memory_space=pltpu.HBM)
    return pl.pallas_call(
        functools.partial(kernel, S, F, R),
        out_shape=pltpu.VMEM((total_rows, cols), bf16),
        in_specs=[hbm] * 13,
        out_specs=vmem,
        scratch_shapes=[
            pltpu.VMEM(queries.shape, bf16), pltpu.VMEM(decoded_key.shape, bf16),
            pltpu.VMEM(decoded_value.shape, bf16),
            pltpu.SMEM(lengths.shape, jnp.int32), pltpu.SMEM(counts.shape, jnp.int32),
            pltpu.VMEM(residual.shape, bf16), pltpu.VMEM(norm_gain.shape, bf16),
            pltpu.VMEM((rows_q, span, kv_width), bf16),
            pltpu.VMEM((rows_q, span, kv_width), bf16),
            pltpu.VMEM((OUT_CHUNKS, out_rows, cols), bf16),
            pltpu.VMEM((PN, *turned), bf16),
            pltpu.VMEM((PN, unit, seg_cols), bf16),
            pltpu.VMEM((rows_q, QUERY_HEADS, HEAD_WIDTH), f32),
            pltpu.VMEM((rows_q, QUERY_HEADS, kv_width), bf16),
            pltpu.VMEM((F, rows_q, QUERY_HEADS, HEAD_WIDTH), bf16),
            pltpu.VMEM((F, rows_q, 8, 128), f32),
            pltpu.VMEM((QUERY_HEADS, HEAD_WIDTH), f32),
            pltpu.VMEM((SR, rows_q, 1, QUERY_HEADS * HEAD_WIDTH), bf16),
            pltpu.VMEM((total_rows, QUERY_HEADS * HEAD_WIDTH), f32),
            pltpu.VMEM((R, total_rows, pl.cdiv(cols, 128) * 128 + 128), bf16),
            *[pltpu.VMEM((F, total_rows, pair + 128), bf16) for _ in range(4)],
            pltpu.VMEM((PN, total_rows, unit), bf16),
            pltpu.VMEM((R, total_rows, cols), bf16),
            pltpu.VMEM((R, total_rows, cols), bf16),
            dma((7,)), dma((rows_q,)), dma((rows_q,)), dma((OUT_CHUNKS,)),
            dma((2 * PN,)), dma((PN,)),
            dma((F, rows_q)), dma((F, rows_q)), dma((F, rows_q)), dma((F, rows_q)),
            dma((SR, rows_q)), dma((SR, rows_q)),
            dma((R,)), dma((R,)), dma((F,)), dma((F,)), dma((F,)), dma((F,)), dma((PN,)), dma((PN,)),
            dma((R,)), dma((R,)),
        ],
        compiler_params=pltpu.CompilerParams(
            collective_id=0, has_side_effects=True, vmem_limit_bytes=65000000
        ),
        name="decode_step",
    )(queries, decoded_key, decoded_value, lengths, counts, residual,
      norm_gain, key_cache, value_cache, out_weight, gate_weight, up_weight,
      down_weight)


def solution(mesh):
    S, F, R = mesh.shape["side"], mesh.shape["ffn"], mesh.shape["rep"]
    return jax.shard_map(
        functools.partial(body, S, F, R),
        mesh=mesh,
        in_specs=(
            P(("groups", "side", "rep"), None),
            P(("groups", "side", "rep"), "ffn", None),
            P(("groups", "side", "rep"), "ffn", None),
            P(("groups", "side", "rep"), None),
            P(("groups", "side", "rep"), None),
            P(("groups", "side", "rep")),
            P("groups"),
            P("groups", ("side", "ffn", "rep")),
            P(None, ("side", "ffn", "rep")),
            P(("side", "ffn", "rep")),
            P("rep", ("side", "ffn")),
            P("rep", ("side", "ffn")),
            P("rep", ("side", "ffn")),
        ),
        out_specs=P("groups", ("side", "ffn", "rep")),
        check_vma=False,
    )
```

```python
import functools

import jax
import jax.numpy as jnp
from jax import lax
from jax.experimental import pallas as pl
from jax.experimental.pallas import tpu as pltpu
from jax.sharding import PartitionSpec as P

D = 8192
QUERY_HEADS = 64
KEY_VALUE_HEADS = 8
HEAD_WIDTH = 128
GROUP_WIDTH = QUERY_HEADS // KEY_VALUE_HEADS
OUT_CHUNKS = 4
TURN_COLS = 256
WO_AT = 2
TURNS = ((0, 2), (2, 4), (4, 6))

norm_eps = 1e-05
MESH = pl.DeviceIdType.MESH
NT = (((1,), (1,)), ((), ()))
f32 = jnp.float32
bf16 = jnp.bfloat16


def kernel(
    S, F, R,
    q_hbm, dk_hbm, dv_hbm, len_hbm, cnt_hbm, res_hbm, gain_hbm,
    k_hbm, v_hbm, wo_hbm, wg_hbm, wu_hbm, wd_hbm,
    out_ref,
    q_ref, dk_ref, dv_ref, len_ref, cnt_ref, res_ref, gain_ref,
    k_v, v_v, wo_v, wt_v, wd_v,
    q_rows, qbd, acc_buf, stat_buf, att_rows, att_buf, att_full,
    y_buf, pre,
    sib_send, sib_recv, gu_send, gu_recv, hid, d_send, d_recv,
    small_sem, k_sem, v_sem, wo_sem, raw_sem, wd_sem,
    acc_ss, acc_rs, stat_ss, stat_rs, att_ss, att_rs,
    y_ss, y_rs,
    sib_ss, sib_rs, gu_ss, gu_rs, hid_ss, hid_rs, d_ss, d_rs,
):
    s = lax.axis_index("side")
    f = lax.axis_index("ffn")
    r = lax.axis_index("rep")
    PN = S * F
    SR = S * R
    me = s * F + f
    mine = s * R + r
    rows_q = q_ref.shape[0]
    span = k_v.shape[1]
    total_rows, cols = res_ref.shape
    kv_width = KEY_VALUE_HEADS * HEAD_WIDTH
    unit, seg_cols = wd_v.shape[1:]
    turn = unit % 128 == 0 and seg_cols % 128 == 0
    pair = gu_recv.shape[2] - 128
    up_at = pair // 2
    ahead = PN // 2
    out_rows = wo_v.shape[1]
    scale = HEAD_WIDTH ** (-0.5)

    def dev(side, ffn, rep):
        return {"side": side, "ffn": ffn, "rep": rep}

    def remote(src, dst, ss, rs, to):
        return pltpu.make_async_remote_copy(
            src_ref=src, dst_ref=dst, send_sem=ss, recv_sem=rs, device_id=to, device_id_type=MESH
        )

    def k_copy(i):
        return pltpu.make_async_copy(k_hbm.at[i], k_v.at[i], k_sem.at[i])

    def v_copy(i):
        return pltpu.make_async_copy(v_hbm.at[i], v_v.at[i], v_sem.at[i])

    def wo_copy(i):
        return pltpu.make_async_copy(
            wo_hbm.at[pl.ds(i * out_rows, out_rows)], wo_v.at[i], wo_sem.at[i]
        )

    def unit_rows(p):
        return pl.ds(pl.multiple_of(p * unit, 8), unit)

    def wd_copy(p):
        return pltpu.make_async_copy(wd_hbm.at[unit_rows(p)], wd_v.at[p], wd_sem.at[p])

    flip = lax.div(2 * f, F)

    def line(j):
        v = F - 1 - j
        up = j + lax.div(j - f + F, F)
        down = v - lax.div(f - v + F, F)
        if isinstance(j, int):
            return f if j == F - 1 else flip * up + (1 - flip) * down
        last = lax.div(j + 1, F)
        return (1 - last) * (flip * up + (1 - flip) * down) + last * f

    lines = [line(j) for j in range(F)]

    def block(own, j):
        side = own * s + (1 - own) * (S - 1 - s)
        ffn = line(j)
        return side, ffn, side * F + ffn

    def in_turn(q):
        q = q + lax.div(q + 3, PN) - 2 * lax.div(q + 2, PN) + lax.div(q + 1, PN)
        last = lax.div(q + 1, PN)
        own = (1 - lax.rem(q, 2)) * lax.div(q + PN - 1, PN) + last
        half = lax.div(q, 2)
        return block(own, own * (half - 1 + last) + (1 - own) * (half + lax.rem(q, 2)))

    def raw_copy(m, t):
        _, _, p = in_turn(t)
        src = (wg_hbm, wu_hbm)[m].at[unit_rows(p)]
        if turn:
            at = 2 * lax.rem(t, ahead) + m
            return pltpu.make_async_copy(src, wd_v.at[at], raw_sem.at[at])
        return pltpu.make_async_copy(src, wt_v.at[p, pl.ds(m * up_at, unit)], raw_sem.at[2 * t + m])

    def turn_pair(t, c):
        _, _, p = in_turn(t)
        for m in range(2):
            raw_copy(m, t).wait()
            for at in range(0, seg_cols, TURN_COLS):
                wt_v[p, at : at + TURN_COLS, m * up_at : m * up_at + unit] = wd_v[
                    2 * lax.rem(t, ahead) + m, :, at : at + TURN_COLS
                ].T

            @pl.when(t < PN - ahead)
            def _():
                raw_copy(m, t + ahead).start(priority=1)

            @pl.when(t >= PN - ahead)
            def _():
                wd_copy(2 * lax.rem(t, ahead) + m).start(priority=1)

        return c

    def turn_range(lo, hi):
        if turn:
            lax.fori_loop(lo * PN // 8, min(hi * PN // 8, PN - 2), turn_pair, 0)

    def far_first(t):
        side = S - 1 - s if t == PN - 2 else t % 2
        ffn = lines[t // 2]
        return side, ffn, side * F + ffn

    def near_first(t):
        side = s if t % 2 == 0 else S - 1 - s
        ffn = lines[F - 1 - t // 2]
        return side, ffn, side * F + ffn

    small = [
        pltpu.make_async_copy(src, dst, small_sem.at[n])
        for n, (src, dst) in enumerate((
            (q_hbm, q_ref), (dk_hbm, dk_ref), (dv_hbm, dv_ref), (len_hbm, len_ref),
            (cnt_hbm, cnt_ref), (res_hbm, res_ref), (gain_hbm, gain_ref),
        ))
    ]
    small[0].start()
    k_copy(0).start()
    for copy in small[1:4]:
        copy.start()
    v_copy(0).start()
    for i in range(1, rows_q):
        k_copy(i).start()
        v_copy(i).start()
    for copy in small[4:]:
        copy.start()
    barrier = pltpu.get_barrier_semaphore()
    group = S * F * R
    my_id = me * R + r

    def greet(t, c):
        other = lax.rem(my_id + t, group)
        pl.semaphore_signal(
            barrier,
            inc=1,
            device_id=dev(lax.div(other, F * R), lax.rem(lax.div(other, R), F), lax.rem(other, R)),
            device_id_type=MESH,
        )
        return c

    lax.fori_loop(1, group, greet, 0)

    qbd[...] = jnp.zeros(qbd.shape, bf16)
    for copy in small[:4]:
        copy.wait()
    for h in range(QUERY_HEADS):
        pair_of = q_ref[:, h * HEAD_WIDTH : (h + 1) * HEAD_WIDTH].astype(f32)
        for i in range(rows_q):
            q_rows[i, h : h + 1, :] = pair_of[i : i + 1, :]

    start_pos = f * span
    leading = f == 0
    positions = start_pos + lax.broadcasted_iota(jnp.int32, (1, span), 1)
    heads = [
        (slice(b * GROUP_WIDTH, (b + 1) * GROUP_WIDTH), slice(b * HEAD_WIDTH, (b + 1) * HEAD_WIDTH))
        for b in range(KEY_VALUE_HEADS)
    ]
    for i in range(rows_q):
        for at, lanes in heads:
            qbd[i, at, lanes] = q_rows[i, at, :].astype(bf16)

    def acc_copy(to, slot, i):
        return remote(
            acc_buf.at[slot, i], acc_buf.at[slot, i], acc_ss.at[to, i], acc_rs.at[slot, i],
            dev(s, to, r),
        )

    def stat_copy(to, slot, i):
        return remote(
            stat_buf.at[slot, i], stat_buf.at[slot, i], stat_ss.at[to, i], stat_rs.at[slot, i],
            dev(s, to, r),
        )

    for i in range(rows_q):
        fresh = scale * jnp.concatenate(
            [
                jnp.sum(q_rows[i, at, :] * dk_ref[i : i + 1, lanes].astype(f32), axis=-1, keepdims=True)
                for at, lanes in heads
            ],
            axis=0,
        )
        k_copy(i).wait()
        if i == rows_q - 1:
            def start_gu(t, c):
                raw_copy(0, t).start(priority=1)
                raw_copy(1, t).start(priority=1)
                return c

            lax.fori_loop(0, WO_AT if turn else PN, start_gu, 0)
            for n in range(OUT_CHUNKS):
                wo_copy(n).start(priority=1)
            lax.fori_loop(WO_AT if turn else PN, ahead if turn else PN, start_gu, 0)
        sc = lax.dot_general(qbd[i], k_v[i], NT, preferred_element_type=f32) * scale
        sc = sc + jnp.where(positions < len_ref[i], 0.0, -1e30)
        peak = jnp.maximum(jnp.max(sc, axis=-1, keepdims=True), -1e29)
        peak = jnp.where(leading, jnp.maximum(peak, fresh), peak)
        w = jnp.exp(sc - peak)
        wn = jnp.where(leading, jnp.exp(fresh - peak), 0.0)
        norm = jnp.sum(w, axis=-1, keepdims=True) + wn
        both = jnp.broadcast_to(jnp.concatenate([peak, norm], axis=0), (2 * QUERY_HEADS, 128))
        stat_buf[f, i] = both.T[0:8, :]
        v_copy(i).wait()
        o = jnp.dot(w.astype(bf16), v_v[i], preferred_element_type=f32)
        wn = wn.astype(bf16).astype(f32)
        acc_buf[f, i] = jnp.concatenate(
            [o[at, lanes] + wn[at] * dv_ref[i : i + 1, lanes].astype(f32) for at, lanes in heads],
            axis=0,
        ).astype(bf16)
        if i == 0:
            pl.semaphore_wait(barrier, group - 1)

        def send_acc(t, c, i=i):
            to = lax.rem(f + t, F)
            stat_copy(to, f, i).start()
            acc_copy(to, f, i).start()
            return c

        lax.fori_loop(1, F, send_acc, 0)

    if not turn:
        for t in range(PN):
            wd_copy(near_first(t)[2]).start(priority=1)

    turn_range(*TURNS[0])

    def att_copy(other, slot, i):
        return remote(
            att_buf.at[slot, i], att_buf.at[slot, i], att_ss.at[other, i], att_rs.at[slot, i],
            dev(lax.div(other, R), f, lax.rem(other, R)),
        )

    low = lax.broadcasted_iota(jnp.int32, (8, 128), 1) < QUERY_HEADS
    for i in range(rows_q):
        def recv_acc(t, c, i=i):
            src = lax.rem(f + t, F)
            stat_copy(src, src, i).wait_recv()
            acc_copy(src, src, i).wait_recv()
            return c

        lax.fori_loop(1, F, recv_acc, 0)
        stats = [stat_buf[z, i] for z in range(F)]
        top = stats[0]
        for z in range(1, F):
            top = jnp.maximum(top, stats[z])
        factors = [jnp.exp(v - top) for v in stats]
        total = factors[0] * pltpu.roll(stats[0], QUERY_HEADS, 1)
        for z in range(1, F):
            total = total + factors[z] * pltpu.roll(stats[z], QUERY_HEADS, 1)
        total = jnp.where(low, total, 1.0)
        factors = [v / total for v in factors]
        if 8 * F < 128:
            factors.append(jnp.zeros((128 - 8 * F, 128), f32))
        turned = jnp.concatenate(factors, axis=0).T
        attended = turned[:QUERY_HEADS, 0:1] * acc_buf[0, i].astype(f32)
        for z in range(1, F):
            attended = attended + turned[:QUERY_HEADS, 8 * z : 8 * z + 1] * acc_buf[z, i].astype(f32)
        att_rows[...] = attended
        att_buf[mine, i] = jnp.concatenate(
            [att_rows[h : h + 1, :] for h in range(QUERY_HEADS)], axis=1
        ).astype(bf16)

        def send_att(t, c, i=i):
            att_copy(lax.rem(mine + t, SR), mine, i).start()
            return c

        lax.fori_loop(1, SR, send_att, 0)

    turn_range(*TURNS[1])

    for i in range(OUT_CHUNKS):
        wo_copy(i).wait()
    for t in range(SR):
        src = lax.rem(mine + t * R + t * R // SR, SR)
        for i in range(rows_q):
            if t > 0:
                att_copy(src, src, i).wait_recv()
            att_full[pl.ds(src * rows_q + i, 1), :] = att_buf[src, i].astype(f32)
    for copy in small[4:]:
        copy.wait()
    proj = res_ref[...].astype(f32)
    summed = jnp.zeros((total_rows, cols), f32)
    for i in range(OUT_CHUNKS):
        summed = summed + jnp.dot(
            att_full[:, i * out_rows : (i + 1) * out_rows].astype(bf16),
            wo_v[i],
            preferred_element_type=f32,
        )
    stream = (proj + summed).astype(bf16).astype(f32)
    lower = lax.broadcasted_iota(jnp.int32, (total_rows, 128), 1) < 64

    def split(v):
        high = v.astype(bf16).astype(f32)
        return jnp.where(lower, high, v - high).astype(bf16)

    def joined(v):
        v = v.astype(f32)
        return v + pltpu.roll(v, 64, 1)

    sq_at = y_buf.shape[2] - 128
    y_buf[r, :, :cols] = (stream * gain_ref[...].astype(f32).reshape(1, cols)).astype(bf16)
    y_buf[r, :, sq_at:] = split(
        jnp.broadcast_to(jnp.sum(stream * stream, axis=1, keepdims=True), (total_rows, 128))
    )

    def y_copy(to, slot):
        return remote(y_buf.at[slot], y_buf.at[slot], y_ss.at[to], y_rs.at[slot], dev(s, f, to))

    def send_y(t, c):
        to = lax.rem(r + t, R)
        y_copy(to, r).start()
        return c

    lax.fori_loop(1, R, send_y, 0)

    aligned = cols % 128 == 0
    turn_range(*TURNS[2])
    early = turn and aligned and R == 2 and cols % 256 == 0

    def half_of(which, lhs):
        return sum(
            jnp.dot(
                lhs[:, at : at + 256],
                wt_v[
                    block(0, 0)[2], pl.ds(pl.multiple_of(which * cols + at, 256), 256)
                ],
                preferred_element_type=f32,
            )
            for at in range(0, cols, 256)
        )

    if early:
        pre[...] = half_of(r, y_buf[r, :, :cols])

    def recv_y(t, c):
        src = lax.rem(r + t, R)
        y_copy(src, src).wait_recv()
        return c

    lax.fori_loop(1, R, recv_y, 0)
    squares = joined(y_buf[0, :, sq_at:])
    for j in range(1, R):
        squares = squares + joined(y_buf[j, :, sq_at:])

    def place(j):
        a = lax.broadcasted_iota(jnp.int32, (cols, seg_cols), 0)
        b = lax.broadcasted_iota(jnp.int32, (cols, seg_cols), 1)
        return jnp.where(b == a + j * cols, 1.0, 0.0).astype(bf16)

    if aligned:
        segment = jnp.concatenate([y_buf[j, :, :cols] for j in range(R)], axis=1)
    else:
        segment = jnp.zeros((total_rows, seg_cols), f32)
        for j in range(R):
            segment = segment + jnp.dot(y_buf[j, :, :cols], place(j), preferred_element_type=f32)
        segment = segment.astype(bf16)

    def sib_copy(j):
        ffn = line(j)
        return remote(
            sib_send.at[ffn], sib_recv.at[ffn], sib_ss.at[ffn], sib_rs.at[ffn], dev(S - 1 - s, f, r)
        )

    def gu_copy(ffn, own):
        slot = f if own else ffn
        return remote(
            gu_send.at[ffn], gu_recv.at[slot], gu_ss.at[ffn], gu_rs.at[slot], dev(s, ffn, r)
        )

    def hid_copy(t, own):
        side, ffn, p = far_first(t) if own else near_first(t)
        slot = me if own else p
        return remote(
            hid.at[slot], hid.at[slot], hid_ss.at[p], hid_rs.at[slot], dev(side, ffn, r)
        )

    def project(p):
        if turn:
            return sum(
                jnp.dot(segment[:, at : at + 256], wt_v[p, at : at + 256], preferred_element_type=f32)
                for at in range(0, seg_cols, 256)
            )
        return lax.dot_general(segment, wt_v[p], NT, preferred_element_type=f32)

    def wait_raw(q):
        if not turn:
            raw_copy(0, q).wait()
            raw_copy(1, q).wait()

    def project_stored(q, p):
        if not turn:
            wait_raw(q)
            return project(p)
        both = []
        for m in range(2):
            at = 2 * (q % ahead) + m
            raw_copy(m, q).wait()
            both.append(lax.dot_general(segment, wd_v[at], NT, preferred_element_type=f32))
        for m in range(2):
            wd_copy(2 * (q % ahead) + m).start(priority=1)
        return jnp.concatenate(both, axis=1)

    def send_sibling(j, v):
        ffn = lines[j]
        sib_send[ffn, :, :pair] = v.astype(bf16)
        sib_send[ffn, :, pair:] = split(squares)
        sib_copy(j).start()

    def project_far(j, ffn, v):
        sib_copy(j).wait_recv()
        gu_send[ffn, :, :pair] = (v + sib_recv[ffn, :, :pair].astype(f32)).astype(bf16)
        gu_send[ffn, :, pair:] = split(squares + joined(sib_recv[ffn, :, pair:]))
        gu_copy(ffn, True).start()

    def project_both(j, c):
        wait_raw(2 * j + 1)
        wait_raw(2 * j + 2)
        _, sib, p = block(0, j + 1)
        _, ffn, q = block(1, j)
        a = project(p)
        v = project(q)
        sib_send[sib, :, :pair] = a.astype(bf16)
        sib_send[sib, :, pair:] = split(squares)
        sib_copy(j + 1).start()
        project_far(j, ffn, v)
        return c

    wait_raw(0)
    if early:
        send_sibling(0, pre[...] + half_of(1 - r, y_buf[1 - r, :, :cols]))
    else:
        send_sibling(0, project(block(0, 0)[2]))
    lax.fori_loop(0, F - 2, project_both, 0)
    wait_raw(PN - 3)
    _, near, at_near = block(1, F - 2)
    project_far(F - 2, near, project(at_near))
    send_sibling(F - 1, project_stored(PN - 2, block(0, F - 1)[2]))
    sums = project_stored(PN - 1, me)
    sib_copy(F - 1).wait_recv()
    sums = sums + sib_recv[f, :, :pair].astype(f32)
    squares = squares + joined(sib_recv[f, :, pair:])

    for t in range(1, F):
        src = lines[F - 1 - t]
        gu_copy(src, False).wait_recv()
        v = gu_recv[src]
        sums = sums + v[:, :pair].astype(f32)
        squares = squares + joined(v[:, pair:])

    sums = sums * lax.rsqrt(squares / D + norm_eps)[:, 0:1]
    g = sums[:, :unit]
    u = sums[:, up_at : up_at + unit]
    hid[me] = (g / (1.0 + jnp.exp(-g)) * u).astype(bf16)

    for t in range(PN - 1):
        hid_copy(t, True).start()

    def drain_f(t, c):
        to = lax.rem(f + t, F)
        for i in range(rows_q):
            stat_copy(to, f, i).wait_send()
            acc_copy(to, f, i).wait_send()
        gu_copy(to, True).wait_send()
        return c

    lax.fori_loop(1, F, drain_f, 0)

    def drain_sr(t, c):
        for i in range(rows_q):
            att_copy(lax.rem(mine + t, SR), mine, i).wait_send()
        return c

    lax.fori_loop(1, SR, drain_sr, 0)

    def drain_y(t, c):
        y_copy(lax.rem(r + t, R), r).wait_send()
        return c

    lax.fori_loop(1, R, drain_y, 0)

    for j in range(F):
        sib_copy(j).wait_send()

    terms = jnp.zeros((total_rows, seg_cols), f32)
    for t in range(PN):
        p = near_first(t)[2]
        wd_copy(p).wait()
        if t > 0:
            hid_copy(t, False).wait_recv()
        terms = terms + jnp.dot(hid[p], wd_v[p], preferred_element_type=f32)
    terms = terms.astype(bf16)
    for j in range(R):
        if aligned:
            d_send[j] = terms[:, j * cols : (j + 1) * cols]
        else:
            d_send[j] = lax.dot_general(
                terms, place(j), NT, preferred_element_type=f32
            ).astype(bf16)

    def d_copy(to, own):
        return remote(
            d_send.at[to], d_recv.at[r if own else to], d_ss.at[to],
            d_rs.at[r if own else to], dev(s, f, to),
        )

    def send_d(t, c):
        d_copy(lax.rem(r + t, R), True).start()
        return c

    lax.fori_loop(1, R, send_d, 0)

    row = lax.broadcasted_iota(jnp.int32, (total_rows, cols), 0)
    slots = total_rows // cnt_ref.shape[0]
    limit = jnp.zeros((total_rows, cols), jnp.int32)
    for i in range(cnt_ref.shape[0]):
        limit = jnp.where(row // slots == i, cnt_ref[i], limit)
    active = lax.rem(row, slots) < limit

    for t in range(PN - 1):
        hid_copy(t, True).wait_send()

    def recv_d(t, c):
        src = lax.rem(r + t, R)
        d_copy(src, False).wait_recv()
        return c + d_recv[src].astype(f32)

    ffn_out = lax.fori_loop(1, R, recv_d, d_send[r].astype(f32))
    out_ref[...] = jnp.where(active, stream + ffn_out, 0.0).astype(bf16)

    def drain_d(t, c):
        d_copy(lax.rem(r + t, R), True).wait_send()
        return c

    lax.fori_loop(1, R, drain_d, 0)


def body(S, F, R, queries, key_cache, value_cache, decoded_key, decoded_value, lengths, counts,
         residual, out_weight, norm_gain, gate_weight, up_weight, down_weight):
    rows_q = queries.shape[0]
    span = key_cache.shape[1]
    kv_width = key_cache.shape[2]
    total_rows, cols = residual.shape
    units, seg_cols = gate_weight.shape
    PN, SR = S * F, S * R
    unit = units // PN
    turn = unit % 128 == 0 and seg_cols % 128 == 0
    pair = 2 * pl.cdiv(unit, 128) * 128
    turned = (seg_cols, pair) if turn else (pair, seg_cols)
    out_rows = out_weight.shape[0] // OUT_CHUNKS
    dma = pltpu.SemaphoreType.DMA
    vmem = pl.BlockSpec(memory_space=pltpu.VMEM)
    hbm = pl.BlockSpec(memory_space=pltpu.HBM)
    return pl.pallas_call(
        functools.partial(kernel, S, F, R),
        out_shape=pltpu.VMEM((total_rows, cols), bf16),
        in_specs=[hbm] * 13,
        out_specs=vmem,
        scratch_shapes=[
            pltpu.VMEM(queries.shape, bf16), pltpu.VMEM(decoded_key.shape, bf16),
            pltpu.VMEM(decoded_value.shape, bf16),
            pltpu.SMEM(lengths.shape, jnp.int32), pltpu.SMEM(counts.shape, jnp.int32),
            pltpu.VMEM(residual.shape, bf16), pltpu.VMEM(norm_gain.shape, bf16),
            pltpu.VMEM((rows_q, span, kv_width), bf16),
            pltpu.VMEM((rows_q, span, kv_width), bf16),
            pltpu.VMEM((OUT_CHUNKS, out_rows, cols), bf16),
            pltpu.VMEM((PN, *turned), bf16),
            pltpu.VMEM((PN, unit, seg_cols), bf16),
            pltpu.VMEM((rows_q, QUERY_HEADS, HEAD_WIDTH), f32),
            pltpu.VMEM((rows_q, QUERY_HEADS, kv_width), bf16),
            pltpu.VMEM((F, rows_q, QUERY_HEADS, HEAD_WIDTH), bf16),
            pltpu.VMEM((F, rows_q, 8, 128), f32),
            pltpu.VMEM((QUERY_HEADS, HEAD_WIDTH), f32),
            pltpu.VMEM((SR, rows_q, 1, QUERY_HEADS * HEAD_WIDTH), bf16),
            pltpu.VMEM((total_rows, QUERY_HEADS * HEAD_WIDTH), f32),
            pltpu.VMEM((R, total_rows, pl.cdiv(cols, 128) * 128 + 128), bf16),
            pltpu.VMEM((total_rows, pair), f32),
            *[pltpu.VMEM((F, total_rows, pair + 128), bf16) for _ in range(4)],
            pltpu.VMEM((PN, total_rows, unit), bf16),
            pltpu.VMEM((R, total_rows, cols), bf16),
            pltpu.VMEM((R, total_rows, cols), bf16),
            dma((7,)), dma((rows_q,)), dma((rows_q,)), dma((OUT_CHUNKS,)),
            dma((2 * PN,)), dma((PN,)),
            dma((F, rows_q)), dma((F, rows_q)), dma((F, rows_q)), dma((F, rows_q)),
            dma((SR, rows_q)), dma((SR, rows_q)),
            dma((R,)), dma((R,)), dma((F,)), dma((F,)), dma((F,)), dma((F,)), dma((PN,)), dma((PN,)),
            dma((R,)), dma((R,)),
        ],
        compiler_params=pltpu.CompilerParams(
            collective_id=0, has_side_effects=True, vmem_limit_bytes=65000000
        ),
        name="decode_step",
    )(queries, decoded_key, decoded_value, lengths, counts, residual,
      norm_gain, key_cache, value_cache, out_weight, gate_weight, up_weight,
      down_weight)


def solution(mesh):
    S, F, R = mesh.shape["side"], mesh.shape["ffn"], mesh.shape["rep"]
    return jax.shard_map(
        functools.partial(body, S, F, R),
        mesh=mesh,
        in_specs=(
            P(("groups", "side", "rep"), None),
            P(("groups", "side", "rep"), "ffn", None),
            P(("groups", "side", "rep"), "ffn", None),
            P(("groups", "side", "rep"), None),
            P(("groups", "side", "rep"), None),
            P(("groups", "side", "rep")),
            P("groups"),
            P("groups", ("side", "ffn", "rep")),
            P(None, ("side", "ffn", "rep")),
            P(("side", "ffn", "rep")),
            P("rep", ("side", "ffn")),
            P("rep", ("side", "ffn")),
            P("rep", ("side", "ffn")),
        ),
        out_specs=P("groups", ("side", "ffn", "rep")),
        check_vma=False,
    )
```
